32 devices in a mesh: fsdp: 8 (over y, x, core), tp: 4 (over z).
Axes of the slice: x: 2, y: 2, z: 4, core: 2. Of those that a mesh axis runs over, the one named last changes fastest.
Arguments:
- tokens: bfloat16 [8192, 1024], P(('fsdp', 'tp')), may hold values from -6 to 6
- lengths: int32 [8], P('fsdp'), may hold values from 1024 to 1024, as said below
- gain_mix: bfloat16 [1024], P(('tp', 'fsdp')), may hold values from 0.25 to 1.75
- w_query: bfloat16 [1024, 1024], P('fsdp', 'tp'), may hold values from -0.1875 to 0.1875
- w_key: bfloat16 [1024, 1024], P('fsdp', 'tp'), may hold values from -0.1875 to 0.1875
- w_value: bfloat16 [1024, 2048], P('fsdp', 'tp'), may hold values from -0.1875 to 0.1875
- w_outgate: bfloat16 [1024, 2048], P('fsdp', 'tp'), may hold values from -0.1875 to 0.1875
- w_beta: bfloat16 [1024, 8], P('fsdp', 'tp'), may hold values from -0.1875 to 0.1875
- w_decay: bfloat16 [1024, 8], P('fsdp', 'tp'), may hold values from -0.1875 to 0.1875
- conv_query: bfloat16 [4, 1024], P(None, ('tp', 'fsdp')), may hold values from -3 to 3
- conv_key: bfloat16 [4, 1024], P(None, ('tp', 'fsdp')), may hold values from -3 to 3
- conv_value: bfloat16 [4, 2048], P(None, ('tp', 'fsdp')), may hold values from -3 to 3
- decay_log: bfloat16 [8], P('tp'), may hold values from 0 to 2.6875
- decay_bias: bfloat16 [8], P('tp'), may hold values from -6.875 to -2.296875
- gain_head: bfloat16 [256], P(('tp', 'fsdp')), may hold values from 0.25 to 1.75
- w_out: bfloat16 [2048, 1024], P('tp', 'fsdp'), may hold values from -0.25 to 0.25
- gain_ff: bfloat16 [1024], P(('tp', 'fsdp')), may hold values from 0.25 to 1.75
- w_gate: bfloat16 [1024, 2816], P('fsdp', 'tp'), may hold values from -0.1875 to 0.1875
- w_up: bfloat16 [1024, 2816], P('fsdp', 'tp'), may hold values from -0.1875 to 0.1875
- w_down: bfloat16 [2816, 1024], P('tp', 'fsdp'), may hold values from -0.109375 to 0.109375
- cotangent: bfloat16 [8192, 1024], P(('fsdp', 'tp')), may hold values from -6 to 6
Outputs:
- layer_out: bfloat16 [8192, 1024], P(('fsdp', 'tp'))
- input_grad: float32 [8192, 1024], P(('fsdp', 'tp'))
- gain_mix_grad: float32 [1024], P(('tp', 'fsdp'))
- w_query_grad: float32 [1024, 1024], P('fsdp', 'tp')
- w_key_grad: float32 [1024, 1024], P('fsdp', 'tp')
- w_value_grad: float32 [1024, 2048], P('fsdp', 'tp')
- w_outgate_grad: float32 [1024, 2048], P('fsdp', 'tp')
- w_beta_grad: float32 [1024, 8], P('fsdp', 'tp')
- w_decay_grad: float32 [1024, 8], P('fsdp', 'tp')
- conv_query_grad: float32 [4, 1024], P(None, ('tp', 'fsdp'))
- conv_key_grad: float32 [4, 1024], P(None, ('tp', 'fsdp'))
- conv_value_grad: float32 [4, 2048], P(None, ('tp', 'fsdp'))
- decay_log_grad: float32 [8], P('tp')
- decay_bias_grad: float32 [8], P('tp')
- gain_head_grad: float32 [256], P(('tp', 'fsdp'))
- w_out_grad: float32 [2048, 1024], P('tp', 'fsdp')
- gain_ff_grad: float32 [1024], P(('tp', 'fsdp'))
- w_gate_grad: float32 [1024, 2816], P('fsdp', 'tp')
- w_up_grad: float32 [1024, 2816], P('fsdp', 'tp')
- w_down_grad: float32 [2816, 1024], P('tp', 'fsdp')
The draws below stay inside these ranges and needn't reach their ends.
Inputs may be any that keep to these rules, and one draw needn't show every extreme that they name: lengths[g] is how many leading slots of group g hold its sequence; the other slots are padding; at least one group is full.
All inputs are finite; a program needn't handle non-finite values.
Results may differ from the reference program's by a relative error of at most 0.025.
Values may be sent and summed in bfloat16 or wider, within the bound.
A program may use at most 256 MiB of HBM per device.

```python
import jax
import jax.numpy as jnp
from jax import lax

D = 1024
H = 8
DK = 128
DV = 256
FF = 2816
KW = 4
SPAN = 64
PACK = 1024
LEN_MIN = 1024
TOKENS = 8192
N_FSDP = 8


def draw_lengths(key, part):
    first_key, second_key = jax.random.split(key)
    drawn = jax.random.randint(first_key, (N_FSDP,), LEN_MIN, PACK + 1)
    chosen = jax.random.randint(second_key, (), 0, N_FSDP)
    return jnp.where(jnp.arange(N_FSDP) == chosen, PACK, drawn).astype(jnp.int32)


def block_scale(own_key, dims, pieces, low, largest):
    factor_of = 1.0
    for dim, blocks in pieces:
        steps = jax.random.uniform(jax.random.fold_in(jax.random.fold_in(own_key, 6), dim), (blocks,), jnp.float32, low / len(pieces), largest / len(pieces))
        factor_of = factor_of * jnp.repeat(jnp.exp(steps), dims[dim] // blocks).reshape((-1,) + (1,) * (len(dims) - 1 - dim))
    return factor_of


def normal_values(key, extent, deviation, most, cuts=(), held_as=jnp.bfloat16):
    entries = deviation * jax.random.normal(key, extent, jnp.float32)
    if cuts:
        entries = entries * block_scale(key, extent, cuts, -0.22, 0.18)
    return jnp.clip(entries, -most, most).astype(held_as)


def setup_inputs(seed: int = 0) -> dict:
    key_list = jax.random.split(jax.random.key(seed), 22)
    return {
        "tokens": normal_values(key_list[0], (TOKENS, D), 1.0, 6.0, ((0, 32),)),
        "lengths": draw_lengths(jax.random.fold_in(key_list[21], 71), 0),
        "gain_mix": jnp.clip(1.0 + 0.15 * jax.random.normal(key_list[2], (D,), jnp.float32), 0.25, 1.75).astype(jnp.bfloat16),
        "w_query": normal_values(key_list[3], (D, H * DK), D ** -0.5, 0.1875, ((0, 8), (1, 4))),
        "w_key": normal_values(key_list[4], (D, H * DK), D ** -0.5, 0.1875, ((0, 8), (1, 4))),
        "w_value": normal_values(key_list[5], (D, H * DV), D ** -0.5, 0.1875, ((0, 8), (1, 4))),
        "w_outgate": normal_values(key_list[6], (D, H * DV), D ** -0.5, 0.1875, ((0, 8), (1, 4))),
        "w_beta": normal_values(key_list[7], (D, H), D ** -0.5, 0.1875, ((0, 8), (1, 4))),
        "w_decay": normal_values(key_list[8], (D, H), D ** -0.5, 0.1875, ((0, 8), (1, 4))),
        "conv_query": normal_values(key_list[9], (KW, H * DK), KW ** -0.5, 3.0, ((1, 32),)),
        "conv_key": normal_values(key_list[10], (KW, H * DK), KW ** -0.5, 3.0, ((1, 32),)),
        "conv_value": normal_values(key_list[11], (KW, H * DV), KW ** -0.5, 3.0, ((1, 32),)),
        "decay_log": jnp.clip(2.6875 * jax.random.uniform(key_list[12], (H,), jnp.float32) ** block_scale(key_list[12], (H,), ((0, 4),), -0.2, 0.2), 0.0, 2.6875).astype(jnp.bfloat16),
        "decay_bias": jnp.clip(-6.875 + 4.578125 * jax.random.uniform(key_list[13], (H,), jnp.float32) ** block_scale(key_list[13], (H,), ((0, 4),), -0.2, 0.2), -6.875, -2.296875).astype(jnp.bfloat16),
        "gain_head": jnp.clip(1.0 + 0.15 * jax.random.normal(key_list[14], (DV,), jnp.float32), 0.25, 1.75).astype(jnp.bfloat16),
        "w_out": normal_values(key_list[15], (H * DV, D), (H * DV // 4) ** -0.5, 0.25, ((0, 4), (1, 8))),
        "gain_ff": jnp.clip(1.0 + 0.15 * jax.random.normal(key_list[16], (D,), jnp.float32), 0.25, 1.75).astype(jnp.bfloat16),
        "w_gate": normal_values(key_list[17], (D, FF), D ** -0.5, 0.1875, ((0, 8), (1, 4))),
        "w_up": normal_values(key_list[18], (D, FF), D ** -0.5, 0.1875, ((0, 8), (1, 4))),
        "w_down": normal_values(key_list[19], (FF, D), FF ** -0.5, 0.109375, ((0, 4), (1, 8))),
        "cotangent": normal_values(key_list[20], (TOKENS, D), 1.0, 6.0, ((0, 32),)),
    }


@jax.custom_vjp
def low(v):
    return lax.optimization_barrier(v.astype(jnp.bfloat16)).astype(jnp.float32)

@jax.custom_vjp
def low_back(v):
    return v

def low_keep(v):
    return (low(v), None)

def low_pass(kept, grad):
    return (grad,)

def back_keep(v):
    return (v, None)

def back_low(kept, grad):
    return (low(grad),)
low.defvjp(low_keep, low_pass)
low_back.defvjp(back_keep, back_low)
epsilon = 1e-06

def product(left, right):
    return jnp.dot(left, right, precision=lax.Precision.HIGHEST, preferred_element_type=jnp.float32)

def batched(left, right):
    return jnp.einsum('...ij,...jk->...ik', left, right, precision=lax.Precision.HIGHEST)

def norm_scale(values):
    return lax.rsqrt(lax.optimization_barrier(jnp.mean(values * values, axis=-1, keepdims=True)) + epsilon)

def causal_conv(signal, kernel_taps):
    tap_count = kernel_taps.shape[0]
    length = signal.shape[0]
    padded = jnp.concatenate([jnp.zeros((tap_count - 1, signal.shape[1]), jnp.float32), signal], axis=0)
    summed = kernel_taps[0] * signal
    for offset in range(1, tap_count):
        summed = summed + kernel_taps[offset] * padded[tap_count - 1 - offset:tap_count - 1 - offset + length]
    return summed

def prepare(query_proj, key_proj, value_proj, beta_logit, decay_logit, conv_query, conv_key, conv_value, decay_log, decay_bias):
    row_count = query_proj.shape[0]
    head_count = beta_logit.shape[1]
    queries = jax.nn.silu(causal_conv(query_proj, conv_query)).reshape(row_count, head_count, -1)
    keys_raw = jax.nn.silu(causal_conv(key_proj, conv_key)).reshape(row_count, head_count, -1)
    value_rows = jax.nn.silu(causal_conv(value_proj, conv_value)).reshape(row_count, head_count, -1)
    query_rows = queries * lax.rsqrt(lax.optimization_barrier(jnp.sum(queries * queries, axis=-1, keepdims=True)) + epsilon) * queries.shape[-1] ** (-0.5)
    key_rows = keys_raw * lax.rsqrt(lax.optimization_barrier(jnp.sum(keys_raw * keys_raw, axis=-1, keepdims=True)) + epsilon)
    beta_rows = jax.nn.sigmoid(beta_logit)
    decay_rows = -jnp.exp(decay_log) * jax.nn.softplus(decay_logit + decay_bias)
    return (query_rows, key_rows, value_rows, beta_rows, decay_rows)

def span_inverse(system):
    size = system.shape[-1]
    result = jnp.eye(size, dtype=jnp.float32) - system
    power = batched(system, system)
    levels = size.bit_length() - 2
    for level in range(levels):
        result = result + batched(result, power)
        if level + 1 < levels:
            power = batched(power, power)
    return result

def delta_rule(query_rows, key_rows, value_rows, beta_rows, decay_rows, block_size):
    row_count, head_count, key_size = query_rows.shape
    value_size = value_rows.shape[-1]
    blocks = row_count // block_size

    def split(values):
        return values.reshape((blocks, block_size) + values.shape[1:])
    queries, keys_all, values_all = (split(query_rows), split(key_rows), split(value_rows))
    betas, decays = (split(beta_rows), split(decay_rows))
    cumulative = jnp.cumsum(decays, axis=1)
    cum_heads = jnp.transpose(cumulative, (0, 2, 1))
    betas_heads = jnp.transpose(betas, (0, 2, 1))
    index = jnp.arange(block_size)
    strict = (index[:, None] > index[None, :])[None, None]
    within = (index[:, None] >= index[None, :])[None, None]
    spread = cum_heads[:, :, :, None] - cum_heads[:, :, None, :]
    strict_decay = jnp.where(strict, jnp.exp(jnp.where(strict, spread, 0.0)), 0.0)
    within_decay = jnp.where(within, jnp.exp(jnp.where(within, spread, 0.0)), 0.0)
    key_gram = jnp.einsum('nihd,njhd->nhij', keys_all, keys_all, precision=lax.Precision.HIGHEST)
    system = betas_heads[:, :, :, None] * strict_decay * key_gram
    inverse = span_inverse(system)
    growth = jnp.exp(cumulative)
    weighted_keys = jnp.einsum('nhij,njhd->nhid', inverse, keys_all * (betas * growth)[..., None], precision=lax.Precision.HIGHEST)
    weighted_values = jnp.einsum('nhij,njhv->nhiv', inverse, values_all * betas[..., None], precision=lax.Precision.HIGHEST)
    scores = within_decay * jnp.einsum('nihd,njhd->nhij', queries, keys_all, precision=lax.Precision.HIGHEST)
    scaled_queries = queries * growth[..., None]
    last_sum = cum_heads[:, :, -1]
    tails = jnp.exp(last_sum[:, :, None] - cum_heads)

    def advance(state, block_data):
        w_keys, w_values, block_scores, s_queries, block_keys, block_tail, block_last = block_data
        update = w_values - jnp.einsum('hid,hvd->hiv', w_keys, state, precision=lax.Precision.HIGHEST)
        output = jnp.einsum('ihd,hvd->ihv', s_queries, state, precision=lax.Precision.HIGHEST)
        output = output + jnp.einsum('hij,hjv->ihv', block_scores, update, precision=lax.Precision.HIGHEST)
        state = jnp.exp(block_last)[:, None, None] * state + jnp.einsum('hjv,jhd->hvd', update * block_tail[..., None], block_keys, precision=lax.Precision.HIGHEST)
        return (state, output)
    initial = jnp.zeros((head_count, value_size, key_size), jnp.float32)
    final_state, outputs = lax.scan(jax.checkpoint(advance), initial, (weighted_keys, weighted_values, scores, scaled_queries, keys_all, tails, last_sum))
    return outputs.reshape(row_count, head_count, value_size)

def finish(mixed, gate_proj, gain_head):
    row_count, head_count, value_size = mixed.shape
    normed = mixed * norm_scale(mixed) * gain_head
    gated = normed * jax.nn.silu(gate_proj.reshape(row_count, head_count, value_size))
    return gated.reshape(row_count, head_count * value_size)

def group_forward(tokens_f, live, params):
    gain_mix, w_query, w_key, w_value, w_outgate, w_beta, w_decay, conv_query, conv_key, conv_value, decay_log, decay_bias, gain_head, w_out, gain_ff, w_gate, w_up, w_down = params
    normed = low(tokens_f * norm_scale(tokens_f) * gain_mix)
    query_proj = low_back(product(normed, w_query))
    key_proj = low_back(product(normed, w_key))
    value_proj = low_back(product(normed, w_value))
    gate_proj = low_back(product(normed, w_outgate))
    beta_logit = low_back(product(normed, w_beta))
    decay_logit = low_back(product(normed, w_decay))
    query_rows, key_rows, value_rows, beta_rows, decay_rows = prepare(query_proj, key_proj, value_proj, beta_logit, decay_logit, conv_query, conv_key, conv_value, decay_log, decay_bias)
    mixed = delta_rule(low(query_rows), low(key_rows), low(value_rows), beta_rows, decay_rows, SPAN)
    gated = low(finish(mixed, gate_proj, gain_head))
    branch = low_back(product(gated, w_out))
    hidden_state = tokens_f + branch
    sent = low(hidden_state)
    ff_normed = low(sent * norm_scale(sent) * gain_ff)
    gate_act = low_back(product(ff_normed, w_gate))
    up_act = low_back(product(ff_normed, w_up))
    inner = low(jax.nn.silu(gate_act) * up_act)
    ff_branch = low_back(product(inner, w_down))
    return jnp.where(live[:, None], hidden_state + ff_branch, 0.0)

def reference(tokens, lengths, gain_mix, w_query, w_key, w_value, w_outgate, w_beta, w_decay, conv_query, conv_key, conv_value, decay_log, decay_bias, gain_head, w_out, gain_ff, w_gate, w_up, w_down, cotangent):
    params = tuple((weight.astype(jnp.float32) for weight in (gain_mix, w_query, w_key, w_value, w_outgate, w_beta, w_decay, conv_query, conv_key, conv_value, decay_log, decay_bias, gain_head, w_out, gain_ff, w_gate, w_up, w_down)))
    group_tokens = tokens.astype(jnp.float32).reshape(N_FSDP, PACK, D)
    group_cot = cotangent.astype(jnp.float32).reshape(N_FSDP, PACK, D)
    positions = jnp.arange(PACK, dtype=jnp.int32)

    def per_group(carried, item):
        block_tokens, block_length, block_cot = item
        live = positions < block_length

        def forward(inputs, weights):
            return group_forward(inputs, live, weights)
        result, pull = jax.vjp(forward, block_tokens, params)
        token_grad, weight_grads = pull(block_cot)
        carried = jax.tree.map(lambda first, second: first + second, carried, weight_grads)
        return (carried, (result.astype(jnp.bfloat16), token_grad))
    start = jax.tree.map(jnp.zeros_like, params)
    totals, (results, token_grads) = lax.scan(per_group, start, (group_tokens, lengths, group_cot))
    return (results.reshape(TOKENS, D), token_grads.reshape(TOKENS, D), totals[0], totals[1], totals[2], totals[3], totals[4], totals[5], totals[6], totals[7], totals[8], totals[9], totals[10], totals[11], totals[12], totals[13], totals[14], totals[15], totals[16], totals[17])
```

```python
import functools
import jax
import jax.numpy as jnp
from jax import lax
from jax.experimental import pallas as pl
from jax.experimental.pallas import tpu as pltpu
from jax.sharding import PartitionSpec as P

epsilon = 1e-06
CHUNK = 128
F32 = jnp.float32
BF16 = jnp.bfloat16
NN = (((1,), (0,)), ((), ()))
NT = (((1,), (1,)), ((), ()))
TN = (((0,), (0,)), ((), ()))


def mm(left, right, dims=NN):
    return lax.dot_general(left.astype(BF16), right.astype(BF16), dims, preferred_element_type=F32)


def mm_exact(left, right, dims=NN):
    return lax.dot_general(left, right, dims, precision=lax.Precision.HIGHEST, preferred_element_type=F32)


def sigmoid(x):
    return 1.0 / (1.0 + jnp.exp(-x))


def softplus(x):
    return jnp.maximum(x, 0.0) + jnp.log1p(jnp.exp(-jnp.abs(x)))


def grid_index(shape, axis):
    return lax.broadcasted_iota(jnp.int32, shape, axis)


def unit_inverse(system):
    size = system.shape[0]
    row = grid_index(system.shape, 0)
    col = grid_index(system.shape, 1)
    near = (row // 2) == (col // 2)
    result = jnp.where(row == col, 1.0, 0.0) - jnp.where(near, system, 0.0)
    width = 2
    while width < size:
        joined = (row // (2 * width)) == (col // (2 * width))
        apart = (row // width) != (col // width)
        off = jnp.where(joined & apart, system, 0.0)
        result = result - mm(mm(result, off), result)
        width *= 2
    return result


def rows_ext(ext_ref, offset, rows):
    return ext_ref[pl.ds(offset, rows), :]


def conv_rows(ext_ref, taps_ref, rows):
    total = taps_ref[0:1, :] * ext_ref[pl.ds(8, rows), :]
    for offset in range(1, 4):
        total = total + taps_ref[offset : offset + 1, :] * ext_ref[pl.ds(8 - offset, rows), :]
    return total


def unit_rows(values, scale):
    factor = lax.rsqrt(jnp.sum(values * values, axis=-1, keepdims=True) + epsilon)
    return values * factor * scale, factor


def logits_act(logits, misc_ref, heads):
    lane = grid_index(logits.shape, 1)
    decay = misc_ref[0:1, :] * softplus(logits + misc_ref[1:2, :])
    return jnp.where(lane < heads, sigmoid(logits), decay)


def decay_tables(act, heads):
    rows = act.shape[0]
    row = grid_index((rows, rows), 0)
    col = grid_index((rows, rows), 1)
    tri = jnp.where(row >= col, 1.0, 0.0)
    total = mm_exact(tri, act)
    return total, jnp.transpose(total)


MESH = pl.DeviceIdType.MESH


def cost(micros):
    return pl.CostEstimate(flops=0, bytes_accessed=micros * 3000000, transcendentals=0)


def line_barrier(me, size):
    barrier = pltpu.get_barrier_semaphore()

    @pl.when(me > 0)
    def _():
        pl.semaphore_signal(barrier, inc=1, device_id={"tp": me - 1}, device_id_type=MESH)

    @pl.when(me < size - 1)
    def _():
        pl.semaphore_signal(barrier, inc=1, device_id={"tp": me + 1}, device_id_type=MESH)

    pl.semaphore_wait(barrier, jnp.where(me > 0, 1, 0) + jnp.where(me < size - 1, 1, 0))


PIECE = 32


class StreamSum:
    def __init__(self, size, lag, blocks, x_ref, sum_ref, from_left, from_right, to_left, to_right, sl, sr, rl, rr):
        self.size, self.lag, self.blocks = size, lag, blocks
        self.me = lax.axis_index("tp")
        self.x, self.sum = x_ref, sum_ref
        self.from_left, self.from_right, self.to_left, self.to_right = from_left, from_right, to_left, to_right
        self.sl, self.sr, self.rl, self.rr = sl, sr, rl, rr
        self.half = CHUNK // 2 // PIECE
        self.halves = x_ref.shape[0] // (CHUNK // 2)

    def part(self, ref, p):
        return ref.at[pl.ds(pl.multiple_of(p * PIECE, PIECE), PIECE), :]

    def right(self, src, p):
        return pltpu.make_async_remote_copy(
            src_ref=self.part(src, p), dst_ref=self.part(self.from_left, p), send_sem=self.sr.at[p], recv_sem=self.rl.at[p],
            device_id={"tp": jnp.minimum(self.me + 1, self.size - 1)}, device_id_type=MESH)

    def left(self, src, p):
        return pltpu.make_async_remote_copy(
            src_ref=self.part(src, p), dst_ref=self.part(self.from_right, p), send_sem=self.sl.at[p], recv_sem=self.rr.at[p],
            device_id={"tp": jnp.maximum(self.me - 1, 0)}, device_id_type=MESH)

    def order(self, half):
        return half

    def send_own(self, step):
        @pl.when(self.me == 0)
        def _():
            @pl.loop(0, 2 * self.half)
            def _(k):
                self.right(self.x, self.order(2 * step) * self.half + k).start()

        @pl.when(self.me == self.size - 1)
        def _():
            @pl.loop(0, 2 * self.half)
            def _(k):
                self.left(self.x, self.order(2 * step) * self.half + k).start()

    def advance(self, tick):
        me, size, halves = self.me, self.size, self.halves
        hr = tick - 1 - self.lag * me
        hl = tick - 1 - self.lag * (size - 1 - me)
        hf = tick - 1 - self.lag * jnp.maximum(me, size - 1 - me)

        @pl.loop(0, self.half)
        def _(k):
            @pl.when((me > 0) & (hr >= 0) & (hr < halves))
            def _():
                p = hr * self.half + k
                self.right(self.to_right, p).wait_recv()

                @pl.when(me < size - 1)
                def _():
                    self.part(self.to_right, p)[...] = (
                        self.part(self.from_left, p)[...].astype(F32) + self.part(self.x, p)[...].astype(F32)).astype(BF16)
                    self.right(self.to_right, p).start()

            @pl.when((me < size - 1) & (hl >= 0) & (hl < halves))
            def _():
                p = hl * self.half + k
                self.left(self.to_left, p).wait_recv()

                @pl.when(me > 0)
                def _():
                    self.part(self.to_left, p)[...] = (
                        self.part(self.from_right, p)[...].astype(F32) + self.part(self.x, p)[...].astype(F32)).astype(BF16)
                    self.left(self.to_left, p).start()

            @pl.when((hf >= 0) & (hf < halves))
            def _():
                p = hf * self.half + k
                own = self.part(self.x, p)[...].astype(F32)

                @pl.when(me == 0)
                def _():
                    self.part(self.sum, p)[...] = own + self.part(self.from_right, p)[...].astype(F32)

                @pl.when(me == size - 1)
                def _():
                    self.part(self.sum, p)[...] = own + self.part(self.from_left, p)[...].astype(F32)

                @pl.when((me > 0) & (me < size - 1))
                def _():
                    self.part(self.sum, p)[...] = (
                        own + self.part(self.from_left, p)[...].astype(F32) + self.part(self.from_right, p)[...].astype(F32))

    def finish(self, step):
        @pl.when(step == self.blocks - 1)
        def _():
            @pl.loop(self.halves, self.halves + 1 + self.lag * (self.size - 1))
            def _(tick):
                self.advance(tick)

            @pl.loop(0, self.halves * self.half)
            def _(p):
                @pl.when(self.me < self.size - 1)
                def _():
                    self.right(self.to_right, p).wait_send()

                @pl.when(self.me > 0)
                def _():
                    self.left(self.to_left, p).wait_send()


def stream_scratch(rows, width):
    buf = pltpu.VMEM((rows, width), BF16)
    dma = pltpu.SemaphoreType.DMA((rows // PIECE,))
    return [buf, buf, buf, buf, buf, dma, dma, dma, dma]


def fwd_kernel(
    size, lag, heads, dk, dv, proj_ref, taps_ref, misc_ref, gain_ref, out_w_ref, gated_ref, mixed_ref, u_ref, inv_ref, start_ref, sum_ref,
    ext_ref, state_ref, x_ref, *line_refs
):
    rows = CHUNK
    step = pl.program_id(0)
    line = StreamSum(size, lag, pl.num_programs(0), x_ref, sum_ref, *line_refs)
    kw, vw = heads * dk, heads * dv
    conv_w = 2 * kw + vw

    @pl.when(step == 0)
    def _():
        line_barrier(line.me, size)
        ext_ref[0:8, :] = jnp.zeros((8, conv_w), F32)
        state_ref[...] = jnp.zeros_like(state_ref)

    ext_ref[pl.ds(8, rows), :] = proj_ref[:, 0:conv_w]
    conv = conv_rows(ext_ref, taps_ref, rows)
    ext_ref[0:8, :] = ext_ref[pl.ds(rows, 8), :]
    act = conv * sigmoid(conv)
    logits = logits_act(proj_ref[:, conv_w + vw :], misc_ref, heads)
    cum, cum_t = decay_tables(logits, heads)
    row = grid_index((rows, rows), 0)
    col = grid_index((rows, rows), 1)
    for h in range(heads):
        q, _ = unit_rows(act[:, h * dk : (h + 1) * dk], dk ** (-0.5))
        k, _ = unit_rows(act[:, kw + h * dk : kw + (h + 1) * dk], 1.0)
        v = act[:, 2 * kw + h * dv : 2 * kw + (h + 1) * dv].astype(BF16).astype(F32)
        q, k = q.astype(BF16), k.astype(BF16)
        beta = logits[:, h : h + 1]
        g_col = cum[:, heads + h : heads + h + 1]
        g_row = cum_t[heads + h : heads + h + 1, :]
        decay = jnp.where(row >= col, jnp.exp(jnp.where(row >= col, g_col - g_row, 0.0)), 0.0)
        grams = mm(jnp.concatenate([k, q], axis=0), k, NT)
        system = jnp.where(row > col, decay * grams[:rows], 0.0) * beta
        scores = decay * grams[rows:]
        inverse = unit_inverse(system)
        growth = jnp.exp(g_col)
        g_last = g_row[:, rows - 1 : rows]
        tail = jnp.exp(g_last - g_col)
        state = state_ref[:, h * dv : (h + 1) * dv]
        start_ref[0, :, h * dv : (h + 1) * dv] = state.astype(start_ref.dtype)
        seen = mm(jnp.concatenate([k, q], axis=0), state)
        u = mm(inverse, beta * (v - growth * seen[:rows]))
        mixed = growth * seen[rows:] + mm(scores, u)
        state_ref[:, h * dv : (h + 1) * dv] = jnp.exp(g_last) * state + mm(k, tail * u, TN)
        cols = slice(h * dv, (h + 1) * dv)
        mixed_ref[:, cols] = mixed
        u_ref[:, cols] = u.astype(u_ref.dtype)
        inv_ref[:, h * rows : (h + 1) * rows] = inverse.astype(inv_ref.dtype)
        gate = proj_ref[:, conv_w + h * dv : conv_w + (h + 1) * dv]
        scale = lax.rsqrt(jnp.mean(mixed * mixed, axis=-1, keepdims=True) + epsilon)
        gated = (mixed * scale * gain_ref[:, cols] * gate * sigmoid(gate)).astype(BF16)
        gated_ref[:, cols] = gated
        part = mm(gated, out_w_ref[conv_w + vw + 128 + h * dv : conv_w + vw + 128 + (h + 1) * dv, :])
        branch = part if h == 0 else branch + part
        if h == 0:
            line.advance(2 * step)
    x_ref[pl.ds(pl.multiple_of(step * rows, rows), rows), :] = branch.astype(BF16)
    line.send_own(step)
    line.advance(2 * step + 1)
    line.finish(step)


def mixer_fwd(proj, taps, misc, gain, out_w, heads, dk, dv, size, lag, collective_id):
    total_rows, width = proj.shape
    chunks = total_rows // CHUNK
    vw = heads * dv
    conv_w = 2 * heads * dk + vw
    model = out_w.shape[1]
    blk = lambda w: pl.BlockSpec((CHUNK, w), lambda c: (c, 0))
    full = lambda a: pl.BlockSpec(a.shape, lambda c: (0, 0))
    return pl.pallas_call(
        functools.partial(fwd_kernel, size, lag, heads, dk, dv),
        grid=(chunks,),
        in_specs=[blk(width), full(taps), full(misc), full(gain), full(out_w)],
        out_specs=[
            blk(vw), blk(vw), blk(vw), blk(heads * CHUNK), pl.BlockSpec((1, dk, vw), lambda c: (c, 0, 0)),
            pl.BlockSpec((total_rows, model), lambda c: (0, 0)),
        ],
        out_shape=[
            jax.ShapeDtypeStruct((total_rows, vw), BF16),
            jax.ShapeDtypeStruct((total_rows, vw), F32),
            jax.ShapeDtypeStruct((total_rows, vw), BF16),
            jax.ShapeDtypeStruct((total_rows, heads * CHUNK), BF16),
            jax.ShapeDtypeStruct((chunks, dk, vw), BF16),
            jax.ShapeDtypeStruct((total_rows, model), F32),
        ],
        scratch_shapes=[pltpu.VMEM((8 + CHUNK, conv_w), F32), pltpu.VMEM((dk, vw), F32)] + stream_scratch(total_rows, model),
        compiler_params=pltpu.CompilerParams(collective_id=collective_id, has_side_effects=True),
        cost_estimate=cost(65),
        name="mixer_fwd",
    )(proj, taps, misc, gain, out_w)


def bwd_kernel(heads, dk, dv, grad_ref, proj_ref, before_ref, taps_ref, misc_ref, gain_ref, mixed_ref, u_ref, inv_ref, start_ref,
               gproj_ref, tapg_ref, small_ref, gaing_ref, ext_ref, back_ref, dstate_ref):
    rows = CHUNK
    kw, vw = heads * dk, heads * dv
    conv_w = 2 * kw + vw
    step = pl.program_id(0)
    chunk = pl.num_programs(0) - 1 - step

    @pl.when(step == 0)
    def _():
        back_ref[pl.ds(rows, 8), :] = jnp.zeros((8, conv_w), F32)
        dstate_ref[...] = jnp.zeros_like(dstate_ref)
        tapg_ref[...] = jnp.zeros_like(tapg_ref)
        small_ref[...] = jnp.zeros_like(small_ref)
        gaing_ref[...] = jnp.zeros_like(gaing_ref)

    ext_ref[0:8, :] = jnp.where(chunk > 0, before_ref[:, 0:conv_w], 0.0)
    ext_ref[pl.ds(8, rows), :] = proj_ref[:, 0:conv_w]
    conv = conv_rows(ext_ref, taps_ref, rows)
    sig = sigmoid(conv)
    act = conv * sig
    dact = sig * (1.0 + conv * (1.0 - sig))
    raw = proj_ref[:, conv_w + vw :]
    logits = logits_act(raw, misc_ref, heads)
    cum, cum_t = decay_tables(logits, heads)
    row = grid_index((rows, rows), 0)
    col = grid_index((rows, rows), 1)
    lane = col
    dlog = jnp.zeros((rows, rows), F32)
    for h in range(heads):
        cols = slice(h * dv, (h + 1) * dv)
        gate = proj_ref[:, conv_w + h * dv : conv_w + (h + 1) * dv]
        gsig = sigmoid(gate)
        mixed = mixed_ref[:, cols]
        grad = grad_ref[:, cols].astype(F32)
        gain = gain_ref[:, cols]
        scale = lax.rsqrt(jnp.mean(mixed * mixed, axis=-1, keepdims=True) + epsilon)
        unit = mixed * scale
        weighted = grad * gate * gsig
        gaing_ref[0:1, cols] += jnp.sum(weighted * unit, axis=0, keepdims=True)
        gproj_ref[:, conv_w + h * dv : conv_w + (h + 1) * dv] = (grad * gain * unit * gsig * (1.0 + gate * (1.0 - gsig))).astype(BF16)
        pulled = weighted * gain
        d_out = scale * (pulled - unit * jnp.mean(pulled * unit, axis=-1, keepdims=True))
        qs, ks = slice(h * dk, (h + 1) * dk), slice(kw + h * dk, kw + (h + 1) * dk)
        vs = slice(2 * kw + h * dv, 2 * kw + (h + 1) * dv)
        q_f, q_scale = unit_rows(act[:, qs], dk ** (-0.5))
        k_f, k_scale = unit_rows(act[:, ks], 1.0)
        v = act[:, vs].astype(BF16).astype(F32)
        q, k = q_f.astype(BF16), k_f.astype(BF16)
        q32, k32 = q.astype(F32), k.astype(F32)
        beta = logits[:, h : h + 1]
        g_col = cum[:, heads + h : heads + h + 1]
        g_row = cum_t[heads + h : heads + h + 1, :]
        decay = jnp.where(row >= col, jnp.exp(jnp.where(row >= col, g_col - g_row, 0.0)), 0.0)
        grams = mm(jnp.concatenate([k, q], axis=0), k, NT)
        plain = jnp.where(row > col, decay * grams[:rows], 0.0)
        scores = decay * grams[rows:]
        growth = jnp.exp(g_col)
        g_last = g_row[:, rows - 1 : rows]
        tail = jnp.exp(g_last - g_col)
        inverse = inv_ref[:, h * rows : (h + 1) * rows]
        u = u_ref[:, cols]
        start = start_ref[0, :, cols]
        d_end = dstate_ref[:, cols]
        d_end_b = d_end.astype(BF16)
        d_u = mm(scores, d_out, TN) + tail * mm(k, d_end_b)
        d_rhs = mm(inverse, d_u, TN)
        d_seen = -growth * d_rhs
        g_out = growth * d_out
        both = mm(jnp.concatenate([d_rhs, d_out], axis=0), u, NT)
        d_sys = jnp.where(row > col, -both[:rows], 0.0)
        d_scores = jnp.where(row >= col, both[rows:], 0.0)
        dstate_ref[:, cols] = jnp.exp(g_last) * d_end + mm(jnp.concatenate([k, q], axis=0), jnp.concatenate([beta * d_seen, g_out], axis=0), TN)
        pull = mm(jnp.concatenate([d_seen, g_out], axis=0), start, NT)
        d_k_seen, d_q1 = pull[:rows], pull[rows:]
        d_k_tail = tail * mm(u, d_end_b, NT)
        d_qk = d_scores * decay
        d_gram = d_sys * decay * beta
        d_gram = d_gram + jnp.transpose(d_gram)
        near = mm(jnp.concatenate([d_qk, d_gram], axis=0), k)
        d_q = d_q1 + near[:rows]
        d_k = beta * d_k_seen + d_k_tail + near[rows:] + mm(d_qk, q, TN)
        d_v = beta * d_rhs
        seen_dot = jnp.sum(k32 * d_k_seen, axis=-1, keepdims=True)
        tail_dot = jnp.sum(k32 * d_k_tail, axis=-1, keepdims=True)
        sys_plain = d_sys * plain
        d_beta = jnp.sum(sys_plain, axis=-1, keepdims=True) + jnp.sum(d_rhs * v, axis=-1, keepdims=True) + seen_dot
        mixed_terms = sys_plain * beta + d_scores * scores
        d_cum = (
            jnp.sum(mixed_terms, axis=-1, keepdims=True)
            - jnp.sum(jnp.transpose(mixed_terms), axis=-1, keepdims=True)
            + beta * seen_dot
            - tail_dot
            + jnp.sum(q32 * d_q1, axis=-1, keepdims=True)
        )
        d_last = jnp.sum(tail_dot, axis=0, keepdims=True) + jnp.exp(g_last) * jnp.sum(
            jnp.sum(d_end * start.astype(F32), axis=-1, keepdims=True), axis=0, keepdims=True
        )
        d_cum = d_cum + jnp.where(grid_index((rows, 1), 0) == rows - 1, d_last, 0.0)
        dlog = jnp.where(lane == h, d_beta, jnp.where(lane == heads + h, d_cum, dlog))
        q_hat, k_hat = q_f * dk**0.5, k_f
        d_q = d_q * dk ** (-0.5)
        d_qa = q_scale * (d_q - q_hat * jnp.sum(d_q * q_hat, axis=-1, keepdims=True))
        d_ka = k_scale * (d_k - k_hat * jnp.sum(d_k * k_hat, axis=-1, keepdims=True))
        back_ref[0:rows, qs] = d_qa * dact[:, qs]
        back_ref[0:rows, ks] = d_ka * dact[:, ks]
        back_ref[0:rows, vs] = d_v * dact[:, vs]
    tri = jnp.where(row <= col, 1.0, 0.0)
    d_decay = mm_exact(tri, dlog)
    shifted = sigmoid(raw + misc_ref[1:2, :])
    d_raw = jnp.where(lane < heads, dlog * logits * (1.0 - logits), d_decay * misc_ref[0:1, :] * shifted)
    d_raw = jnp.where(lane < 2 * heads, d_raw, 0.0)
    gproj_ref[:, conv_w + vw :] = d_raw.astype(BF16)
    small_ref[0:1, :] += jnp.sum(d_decay * logits, axis=0, keepdims=True)
    small_ref[1:2, :] += jnp.sum(d_raw, axis=0, keepdims=True)
    here = back_ref[0:rows, :]
    total = taps_ref[0:1, :] * here
    tapg_ref[0:1, :] += jnp.sum(here * ext_ref[pl.ds(8, rows), :], axis=0, keepdims=True)
    for offset in range(1, 4):
        total = total + taps_ref[offset : offset + 1, :] * back_ref[pl.ds(offset, rows), :]
        tapg_ref[offset : offset + 1, :] += jnp.sum(here * ext_ref[pl.ds(8 - offset, rows), :], axis=0, keepdims=True)
    gproj_ref[:, 0:conv_w] = total.astype(BF16)
    back_ref[pl.ds(rows, 8), :] = back_ref[0:8, :]


def mixer_bwd(grad, proj, taps, misc, gain, mixed, u, inverse, start, heads, dk, dv):
    total_rows, width = proj.shape
    chunks = total_rows // CHUNK
    conv_w = 2 * heads * dk + heads * dv
    vw = heads * dv
    last = chunks - 1
    blk = lambda w: pl.BlockSpec((CHUNK, w), lambda c: (last - c, 0))
    full = lambda a: pl.BlockSpec(a.shape, lambda c: (0, 0))
    per = CHUNK // 8
    return pl.pallas_call(
        functools.partial(bwd_kernel, heads, dk, dv),
        grid=(chunks,),
        in_specs=[
            blk(vw), blk(width),
            pl.BlockSpec((8, width), lambda c: (jnp.maximum((last - c) * per - 1, 0), 0)),
            full(taps), full(misc), full(gain), blk(vw), blk(vw), blk(heads * CHUNK),
            pl.BlockSpec((1, dk, vw), lambda c: (last - c, 0, 0)),
        ],
        out_specs=[
            blk(width),
            pl.BlockSpec((8, conv_w), lambda c: (0, 0)),
            pl.BlockSpec((8, 128), lambda c: (0, 0)),
            pl.BlockSpec((8, vw), lambda c: (0, 0)),
        ],
        out_shape=[
            jax.ShapeDtypeStruct((total_rows, width), BF16),
            jax.ShapeDtypeStruct((8, conv_w), F32),
            jax.ShapeDtypeStruct((8, 128), F32),
            jax.ShapeDtypeStruct((8, vw), F32),
        ],
        scratch_shapes=[
            pltpu.VMEM((8 + CHUNK, conv_w), F32),
            pltpu.VMEM((CHUNK + 8, conv_w), F32),
            pltpu.VMEM((dk, vw), F32),
        ],
        cost_estimate=cost(27),
        name="mixer_bwd",
    )(grad, proj, proj, taps, misc, gain, mixed, u, inverse, start)


def ff_kernel(
    size, lag, wide, tokens_ref, branch_ref, grad_ref, gain_ref, w_ref, normed_ref, inner_ref, acts_ref, part_ref, gaing_ref, sum_ref, x_ref, *line_refs
):
    rows = CHUNK
    step = pl.program_id(0)
    line = StreamSum(size, lag, pl.num_programs(0), x_ref, sum_ref, *line_refs)

    @pl.when(step == 0)
    def _():
        line_barrier(line.me, size)
        gaing_ref[...] = jnp.zeros_like(gaing_ref)

    hidden = (tokens_ref[...].astype(F32) + branch_ref[...]).astype(BF16).astype(F32)
    scale = lax.rsqrt(jnp.mean(hidden * hidden, axis=-1, keepdims=True) + epsilon)
    unit = hidden * scale
    normed = (unit * gain_ref[...]).astype(BF16)
    normed_ref[...] = normed
    gate = mm(normed, w_ref[0:wide, :], NT)
    up = mm(normed, w_ref[wide : 2 * wide, :], NT)
    sig = sigmoid(gate)
    inner = (gate * sig * up).astype(BF16)
    inner_ref[...] = inner
    part_ref[...] = mm(inner, w_ref[2 * wide : 3 * wide, :]).astype(BF16)
    line.advance(2 * step)
    grad_inner = mm(grad_ref[...], w_ref[2 * wide : 3 * wide, :], NT)
    grad_gate = (grad_inner * up * sig * (1.0 + gate * (1.0 - sig))).astype(BF16)
    grad_up = (grad_inner * gate * sig).astype(BF16)
    acts_ref[:, 0:wide] = grad_gate
    acts_ref[:, wide : 2 * wide] = grad_up
    grad_normed = mm(grad_gate, w_ref[0:wide, :]) + mm(grad_up, w_ref[wide : 2 * wide, :])
    gaing_ref[0:1, :] += jnp.sum(grad_normed * unit, axis=0, keepdims=True)
    pulled = grad_normed * gain_ref[...]
    sent = scale * (pulled - unit * jnp.mean(pulled * unit, axis=-1, keepdims=True))
    x_ref[pl.ds(pl.multiple_of(step * rows, rows), rows), :] = sent.astype(BF16)
    line.send_own(step)
    line.advance(2 * step + 1)
    line.finish(step)


def feed_forward(tokens, branch, grad, gain, w_rows, wide, size, lag, collective_id):
    total_rows, model = tokens.shape
    chunks = total_rows // CHUNK
    blk = lambda w: pl.BlockSpec((CHUNK, w), lambda c: (c, 0))
    full = lambda r, w: pl.BlockSpec((r, w), lambda c: (0, 0))
    return pl.pallas_call(
        functools.partial(ff_kernel, size, lag, wide),
        grid=(chunks,),
        in_specs=[blk(model), blk(model), blk(model), full(1, model), full(3 * wide, model)],
        out_specs=[blk(model), blk(wide), blk(2 * wide), blk(model), full(8, model), full(total_rows, model)],
        out_shape=[
            jax.ShapeDtypeStruct((total_rows, model), BF16),
            jax.ShapeDtypeStruct((total_rows, wide), BF16),
            jax.ShapeDtypeStruct((total_rows, 2 * wide), BF16),
            jax.ShapeDtypeStruct((total_rows, model), BF16),
            jax.ShapeDtypeStruct((8, model), F32),
            jax.ShapeDtypeStruct((total_rows, model), F32),
        ],
        scratch_shapes=stream_scratch(total_rows, model),
        compiler_params=pltpu.CompilerParams(collective_id=collective_id, has_side_effects=True),
        cost_estimate=cost(65),
        name="feed_forward",
    )(tokens, branch, grad, gain, w_rows)


def peer_barrier(fsdp, tp):
    me_f, me_t = lax.axis_index("fsdp"), lax.axis_index("tp")
    barrier = pltpu.get_barrier_semaphore()

    @pl.loop(1, fsdp)
    def _(d):
        pl.semaphore_signal(barrier, inc=1, device_id={"fsdp": (me_f + d) % fsdp}, device_id_type=MESH)

    @pl.loop(1, tp)
    def _(d):
        pl.semaphore_signal(barrier, inc=1, device_id={"tp": (me_t + d) % tp}, device_id_type=MESH)

    pl.semaphore_wait(barrier, fsdp + tp - 2)


def line_gather_kernel(fsdp, size, pieces, x_ref, tile_ref, out_ref, tiles_ref, own_sem, sl, sr, rl, rr, sp, rp, st, rt):
    me = lax.axis_index("tp")
    shard = x_ref.shape[0]
    rows = shard // pieces
    own = pltpu.make_async_copy(x_ref, out_ref.at[pl.ds(pl.multiple_of(me * shard, shard), shard), :], own_sem)
    own.start()
    me_f = lax.axis_index("fsdp")
    tiles_ref[pl.ds(me_f, 1), pl.ds(me, 1)] = tile_ref[...][None, None]
    peer_barrier(fsdp, size)

    def along(d, slot):
        return pltpu.make_async_remote_copy(
            src_ref=tile_ref, dst_ref=tiles_ref.at[me_f, slot], send_sem=st.at[d], recv_sem=rt.at[slot],
            device_id={"tp": (me + d) % size}, device_id_type=MESH)

    def across(d, slot):
        return pltpu.make_async_remote_copy(
            src_ref=tiles_ref.at[me_f], dst_ref=tiles_ref.at[slot], send_sem=sp.at[d], recv_sem=rp.at[slot],
            device_id={"fsdp": (me_f + d) % fsdp}, device_id_type=MESH)

    @pl.loop(1, size)
    def _(d):
        along(d, me).start()

    def region(ref, s, k):
        return ref.at[pl.ds(pl.multiple_of(s * shard + k * rows, rows), rows), :]

    def to_right(src, s, k):
        return pltpu.make_async_remote_copy(
            src_ref=src, dst_ref=region(out_ref, s, k), send_sem=sr.at[s * pieces + k], recv_sem=rl.at[s * pieces + k],
            device_id={"tp": jnp.minimum(me + 1, size - 1)}, device_id_type=MESH)

    def to_left(src, s, k):
        return pltpu.make_async_remote_copy(
            src_ref=src, dst_ref=region(out_ref, s, k), send_sem=sl.at[s * pieces + k], recv_sem=rr.at[s * pieces + k],
            device_id={"tp": jnp.maximum(me - 1, 0)}, device_id_type=MESH)

    for k in range(pieces):
        src = x_ref.at[pl.ds(k * rows, rows), :]

        @pl.when(me < size - 1)
        def _():
            to_right(src, me, k).start()

        @pl.when(me > 0)
        def _():
            to_left(src, me, k).start()

    @pl.loop(1, size)
    def _(d):
        along(d, (me + d) % size).wait_recv()

    @pl.loop(1, fsdp)
    def _(d):
        across(d, me_f).start()

    @pl.loop(0, (size - 1) * pieces)
    def _(t):
        d = t // pieces + 1
        k = t % pieces
        s_left, s_right = me - d, me + d

        @pl.when(s_left >= 0)
        def _():
            to_right(region(out_ref, s_left, k), s_left, k).wait_recv()

            @pl.when(me < size - 1)
            def _():
                to_right(region(out_ref, s_left, k), s_left, k).start()

        @pl.when(s_right < size)
        def _():
            to_left(region(out_ref, s_right, k), s_right, k).wait_recv()

            @pl.when(me > 0)
            def _():
                to_left(region(out_ref, s_right, k), s_right, k).start()

    own.wait()

    @pl.loop(1, fsdp)
    def _(d):
        across(d, (me_f + d) % fsdp).wait_recv()

    @pl.loop(1, size)
    def _(d):
        along(d, me).wait_send()

    @pl.loop(1, fsdp)
    def _(d):
        across(d, me_f).wait_send()

    @pl.loop(0, size * pieces)
    def _(t):
        s, k = t // pieces, t % pieces

        @pl.when((me < size - 1) & (s <= me))
        def _():
            to_right(region(out_ref, s, k), s, k).wait_send()

        @pl.when((me > 0) & (s >= me))
        def _():
            to_left(region(out_ref, s, k), s, k).wait_send()


def line_gather(x, tile, fsdp, size, pieces, collective_id):
    vm = pl.BlockSpec(memory_space=pltpu.VMEM)
    dma = pltpu.SemaphoreType.DMA((size * pieces,))
    plane, line = pltpu.SemaphoreType.DMA((fsdp,)), pltpu.SemaphoreType.DMA((size,))
    return pl.pallas_call(
        functools.partial(line_gather_kernel, fsdp, size, pieces),
        out_shape=[
            jax.ShapeDtypeStruct((size * x.shape[0], x.shape[1]), x.dtype),
            jax.ShapeDtypeStruct((fsdp, size) + tile.shape, tile.dtype),
        ],
        in_specs=[vm, vm], out_specs=[vm, vm],
        scratch_shapes=[pltpu.SemaphoreType.DMA, dma, dma, dma, dma, plane, plane, line, line],
        compiler_params=pltpu.CompilerParams(collective_id=collective_id, has_side_effects=True),
        cost_estimate=cost(40),
        name="line_gather",
    )(x, tile)


class PlaneSum:
    def __init__(self, n, order, cols, src_ref, out_ref, acc_ref, recv_ref, send_sem, recv_sem):
        self.n, self.order, self.cols = n, order, cols
        self.stages = len(order)
        self.me = lax.axis_index("fsdp")
        self.block = src_ref.shape[0] // n
        self.src, self.out, self.acc, self.recv = src_ref, out_ref, acc_ref, recv_ref
        self.send_sem, self.recv_sem = send_sem, recv_sem

    def bit(self, b):
        return (self.me // b) % 2

    def owner(self, stage, i, flip):
        total = 0
        for b in self.order[:stage]:
            total = total + self.bit(b) * b
        b = self.order[stage]
        total = total + ((1 - self.bit(b)) if flip else self.bit(b)) * b
        for j, r in enumerate(self.order[stage + 1 :]):
            total = total + ((i // (2**j)) % 2) * r
        return total

    def place(self, pair):
        total = 0
        for j, r in enumerate(self.order[1:]):
            total = total + ((pair // (r // 2)) % 2) * 2**j
        return total

    def rows(self, g):
        return pl.ds(pl.multiple_of(g * self.block, self.block), self.block)

    def copy(self, stage, i):
        b = self.order[stage]
        src = self.src if stage == 0 else self.acc
        slot = self.n - (self.n >> stage) + i
        return pltpu.make_async_remote_copy(
            src_ref=src.at[self.rows(self.owner(stage, i, True)), self.cols], dst_ref=self.recv.at[self.rows(slot), self.cols],
            send_sem=self.send_sem.at[slot], recv_sem=self.recv_sem.at[slot],
            device_id={"fsdp": self.me + b - 2 * b * self.bit(b)}, device_id_type=MESH)

    def total(self, stage, i):
        self.copy(stage, i).wait_recv()
        g = self.owner(stage, i, False)
        slot = self.n - (self.n >> stage) + i
        src = self.src if stage == 0 else self.acc
        return g, src[self.rows(g), self.cols].astype(F32) + self.recv[self.rows(slot), self.cols].astype(F32)

    def advance(self, stage):
        if stage == self.stages - 1:
            _, total = self.total(stage, 0)
            self.out[:, self.cols] = total
            return
        mine = self.bit(self.order[stage + 1])
        for flip in (True, False):
            @pl.loop(0, self.n >> (stage + 2))
            def _(i):
                g, total = self.total(stage, 2 * i + (1 - mine if flip else mine))
                self.acc[self.rows(g), self.cols] = total.astype(BF16)
                if flip:
                    self.copy(stage + 1, i).start()

    def finish(self):
        @pl.loop(0, self.n // 2)
        def _(i):
            self.copy(0, i).wait_send()

        for stage in range(1, self.stages):
            @pl.loop(0, self.n >> (stage + 1))
            def _(i):
                self.copy(stage, i).wait_send()


def halving_orders(n):
    bits = [2**j for j in range(n.bit_length() - 1)]
    return bits, bits[:1] + bits[:0:-1]


def last_kernel(
    fsdp, size, pieces, slack, gproj_ref, w_ref, normed_ref, tokens_ref, gain_ref, gbranch_ref, gated_ref, base_ref, small_ref, tapg_ref,
    out_ref, small_out, tap_out, shard_ref,
    x_ref, grads, acc, recv, small, small_in, small_line, tap_in, from_left, from_right, to_left, to_right,
    sl, sr, rl, rr, sp, rp, st, rt, sk, rk, sa, ra, sb, rb
):
    me, me_f = lax.axis_index("tp"), lax.axis_index("fsdp")
    shard = x_ref.shape[0] // size
    rows = shard // pieces
    count = (size - 1) * pieces
    proj_w = gproj_ref.shape[1]
    peer_barrier(fsdp, size)

    def across(d, slot):
        return pltpu.make_async_remote_copy(
            src_ref=small, dst_ref=small_in.at[slot], send_sem=sp.at[d], recv_sem=rp.at[slot],
            device_id={"fsdp": (me_f + d) % fsdp}, device_id_type=MESH)

    def taps_across(d, slot):
        return pltpu.make_async_remote_copy(
            src_ref=tapg_ref, dst_ref=tap_in.at[slot], send_sem=sk.at[d], recv_sem=rk.at[slot],
            device_id={"fsdp": (me_f + d) % fsdp}, device_id_type=MESH)

    def along(d, slot):
        return pltpu.make_async_remote_copy(
            src_ref=small_out, dst_ref=small_line.at[slot], send_sem=st.at[d], recv_sem=rt.at[slot],
            device_id={"tp": (me + d) % size}, device_id_type=MESH)

    width = grads.shape[1]
    cut = (width // 256 + width // 128 % 2) * 128
    order_a, order_b = halving_orders(fsdp)
    planes = [
        PlaneSum(fsdp, order_a, slice(0, cut), grads, shard_ref, acc, recv, sa, ra),
        PlaneSum(fsdp, order_b, slice(cut, width), grads, shard_ref, acc, recv, sb, rb),
    ]

    def part(ref, s, k):
        return ref.at[pl.ds(pl.multiple_of(s * shard + k * rows, rows), rows), :]

    def right_copy(src, s, k):
        return pltpu.make_async_remote_copy(
            src_ref=part(src, s, k), dst_ref=part(from_left, s, k), send_sem=sr.at[s * pieces + k], recv_sem=rl.at[s * pieces + k],
            device_id={"tp": jnp.minimum(me + 1, size - 1)}, device_id_type=MESH)

    def left_copy(src, s, k):
        return pltpu.make_async_remote_copy(
            src_ref=part(src, s, k), dst_ref=part(from_right, s, k), send_sem=sl.at[s * pieces + k], recv_sem=rr.at[s * pieces + k],
            device_id={"tp": jnp.maximum(me - 1, 0)}, device_id_type=MESH)

    def exchange(t):
        ir = t - (me - 1) * slack
        il = t - (size - 2 - me) * slack
        s_r, k_r = size - 1 - ir // pieces, ir % pieces
        s_l, k_l = il // pieces, il % pieces

        @pl.when((me > 0) & (ir >= 0) & (ir < count) & (s_r >= me))
        def _():
            right_copy(to_right, s_r, k_r).wait_recv()

            @pl.when(s_r > me)
            def _():
                part(to_right, s_r, k_r)[...] = (
                    part(from_left, s_r, k_r)[...].astype(F32) + part(x_ref, s_r, k_r)[...].astype(F32)).astype(BF16)
                right_copy(to_right, s_r, k_r).start()

        @pl.when((me < size - 1) & (il >= 0) & (il < count) & (s_l <= me))
        def _():
            left_copy(to_left, s_l, k_l).wait_recv()

            @pl.when(s_l < me)
            def _():
                part(to_left, s_l, k_l)[...] = (
                    part(from_right, s_l, k_l)[...].astype(F32) + part(x_ref, s_l, k_l)[...].astype(F32)).astype(BF16)
                left_copy(to_left, s_l, k_l).start()

    small[...] = small_ref[...]

    @pl.loop(0, size)
    def _(j):
        s = (j % 2) * (j // 2) + (1 - j % 2) * (size - 1 - j // 2)
        here = pl.ds(pl.multiple_of(s * shard, shard), shard)
        grad_normed = mm(gproj_ref[here, :], w_ref[0:proj_w, :])
        values = tokens_ref[here, :].astype(F32)
        scale = lax.rsqrt(jnp.mean(values * values, axis=-1, keepdims=True) + epsilon)
        unit = values * scale
        small[0:1, :] += jnp.sum(grad_normed * unit, axis=0, keepdims=True)
        pulled = grad_normed * gain_ref[...]
        x_ref[here, :] = (scale * (pulled - unit * jnp.mean(pulled * unit, axis=-1, keepdims=True))).astype(BF16)

        @pl.when((me == 0) & (s > 0))
        def _():
            @pl.loop(0, pieces)
            def _(k):
                right_copy(x_ref, s, k).start()

        @pl.when((me == size - 1) & (s < size - 1))
        def _():
            @pl.loop(0, pieces)
            def _(k):
                left_copy(x_ref, s, k).start()

    @pl.loop(1, fsdp)
    def _(d):
        taps_across(d, me_f).start()
        across(d, me_f).start()

    block = grads.shape[0] // fsdp
    many = max(256 // block, 2)
    groups = fsdp // many
    ticks = count + (size - 2) * slack
    per = max(ticks // (3 * groups), 1)

    @pl.loop(0, groups)
    def _(i):
        here = pl.ds(pl.multiple_of(i * many * block, many * block), many * block)
        grads[here, 0:proj_w] = mm(normed_ref[here, :], gproj_ref[...]).astype(BF16)
        grads[here, proj_w:width] = mm(gbranch_ref[here, :], gated_ref[...]).astype(BF16)

        @pl.loop(0, many // 2)
        def _(m):
            for plane in planes:
                plane.copy(0, plane.place(i * (many // 2) + m)).start()

        @pl.loop(i * per, (i + 1) * per)
        def _(t):
            exchange(t)

    stages = len(order_a)
    done = groups * per
    for stage in range(stages):
        until = max(done, int(ticks * (0.4 + 0.45 * stage / max(stages - 1, 1))))

        @pl.loop(done, until)
        def _(t):
            exchange(t)

        done = until
        for plane in planes:
            plane.advance(stage)
        if stage == 0:
            small_out[...] = small[...]
            tap_out[...] = tapg_ref[...]

            @pl.loop(1, fsdp)
            def _(d):
                slot = (me_f + d) % fsdp
                across(d, slot).wait_recv()
                taps_across(d, slot).wait_recv()
                small_out[...] += small_in[pl.ds(slot, 1)][0]
                tap_out[...] += tap_in[pl.ds(slot, 1)][0]

            @pl.loop(1, size)
            def _(d):
                along(d, me).start()

    @pl.loop(done, ticks)
    def _(t):
        exchange(t)

    for plane in planes:
        plane.finish()

    @pl.loop(1, size)
    def _(d):
        along(d, me).wait_send()

    @pl.loop(1, size)
    def _(d):
        slot = (me + d) % size
        along(d, slot).wait_recv()
        small_out[...] += small_line[pl.ds(slot, 1)][0]

    @pl.loop(1, fsdp)
    def _(d):
        across(d, me_f).wait_send()
        taps_across(d, me_f).wait_send()

    @pl.loop(0, pieces)
    def _(k):
        here = pl.ds(pl.multiple_of(k * rows, rows), rows)
        total = base_ref[here, :] + part(x_ref, me, k)[...].astype(F32)

        @pl.when(me == 0)
        def _():
            out_ref[here, :] = total + part(from_right, me, k)[...].astype(F32)

        @pl.when(me == size - 1)
        def _():
            out_ref[here, :] = total + part(from_left, me, k)[...].astype(F32)

        @pl.when((me > 0) & (me < size - 1))
        def _():
            out_ref[here, :] = total + part(from_left, me, k)[...].astype(F32) + part(from_right, me, k)[...].astype(F32)

    @pl.loop(0, size * pieces)
    def _(i):
        s, k = i // pieces, i % pieces

        @pl.when(s > me)
        def _():
            right_copy(to_right, s, k).wait_send()

        @pl.when(s < me)
        def _():
            left_copy(to_left, s, k).wait_send()


def last_sums(gproj, w_rows, normed_t, tokens, gain, gbranch_t, gated, base, small, tapg, fsdp, size, pieces, slack, collective_id):
    vm = pl.BlockSpec(memory_space=pltpu.VMEM)
    total_rows, model = tokens.shape
    width = gproj.shape[1] + gated.shape[1]
    buf = pltpu.VMEM((total_rows, model), BF16)
    pack = pltpu.VMEM((model, width), BF16)
    dma = pltpu.SemaphoreType.DMA((size * pieces,))
    plane, line = pltpu.SemaphoreType.DMA((fsdp,)), pltpu.SemaphoreType.DMA((size,))
    return pl.pallas_call(
        functools.partial(last_kernel, fsdp, size, pieces, slack),
        out_shape=[
            jax.ShapeDtypeStruct(base.shape, F32), jax.ShapeDtypeStruct(small.shape, F32), jax.ShapeDtypeStruct(tapg.shape, F32),
            jax.ShapeDtypeStruct((model // fsdp, width), F32),
        ],
        in_specs=[vm] * 10, out_specs=[vm] * 4,
        scratch_shapes=[
            buf, pack, pack, pack, pltpu.VMEM(small.shape, F32), pltpu.VMEM((fsdp,) + small.shape, F32), pltpu.VMEM((size,) + small.shape, F32),
            pltpu.VMEM((fsdp,) + tapg.shape, F32), buf, buf, buf, buf,
            dma, dma, dma, dma, plane, plane, line, line, plane, plane, plane, plane, plane, plane,
        ],
        compiler_params=pltpu.CompilerParams(collective_id=collective_id, has_side_effects=True),
        cost_estimate=cost(55),
        name="last_sums",
    )(gproj, w_rows, normed_t, tokens, gain, gbranch_t, gated, base, small, tapg)


def norm_scale(values):
    return lax.rsqrt(jnp.mean(values * values, axis=-1, keepdims=True) + epsilon)


def norm_back(grad_normed, values, scale, gain):
    unit = values * scale
    gain_grad = jnp.sum(grad_normed * unit, axis=0)
    pulled = grad_normed * gain
    input_part = scale * (pulled - unit * jnp.mean(pulled * unit, axis=-1, keepdims=True))
    return (input_part, gain_grad)


def body(
    tokens, lengths, gain_mix, w_query, w_key, w_value, w_outgate, w_beta, w_decay,
    conv_query, conv_key, conv_value, decay_log, decay_bias, gain_head, w_out, gain_ff,
    w_gate, w_up, w_down, cotangent,
):
    fsdp, tp = lax.axis_size("fsdp"), lax.axis_size("tp")
    my_fsdp, my_tp = lax.axis_index("fsdp"), lax.axis_index("tp")
    shard_rows, d_model = tokens.shape
    w_rows = w_query.shape[0]
    heads = w_beta.shape[1]
    kw, vw = w_query.shape[1], w_value.shape[1]
    dk, dv = kw // heads, vw // heads
    conv_w = 2 * kw + vw
    main_w = conv_w + vw
    proj_w = main_w + 128
    ff = w_gate.shape[1]
    taps_n = conv_query.shape[0]

    taps_local = jnp.concatenate([conv_query, conv_key, conv_value], axis=1).reshape(1, -1)
    spare = 128 - 2 * heads
    tap_rows = -(-taps_local.shape[1] // spare)
    taps_pack = jnp.pad(taps_local, ((0, 0), (0, tap_rows * spare - taps_local.shape[1]))).reshape(tap_rows, spare)
    taps_pack = jnp.pad(taps_pack, ((0, w_rows - tap_rows), (0, 0)))
    extras = jnp.concatenate([w_beta, w_decay, taps_pack], axis=1)
    mix_pack = jnp.concatenate([jnp.transpose(a) for a in (w_query, w_key, w_value, w_outgate, extras)] + [w_out], axis=0)
    mix_pack, tokens = lax.optimization_barrier((mix_pack, tokens))
    mix_full = lax.all_gather(mix_pack, "fsdp", axis=1, tiled=True)
    n_mix, n_head = gain_mix.shape[0], gain_head.shape[0]
    gains_local = jnp.concatenate([gain_mix, gain_head, gain_ff]).astype(F32)
    gains_tile = jnp.pad(gains_local[None, :], ((0, 7), (0, 128 - gains_local.shape[0])))
    group_tokens, gains = line_gather(tokens, gains_tile, fsdp, tp, 2, 4)
    gains = jnp.transpose(gains[:, :, 0, :], (1, 0, 2)).reshape(tp * fsdp, 128)
    mix_gain = gains[:, :n_mix].reshape(-1)
    head_gain = gains[:, n_mix : n_mix + n_head].reshape(-1)
    ff_gain = gains[:, n_mix + n_head : 2 * n_mix + n_head].reshape(-1)
    live = my_tp * shard_rows + jnp.arange(shard_rows, dtype=jnp.int32) < lengths[0]
    grad_out = jnp.where(live[:, None], cotangent, jnp.zeros_like(cotangent))
    grad_out, group_tokens, mix_full = lax.optimization_barrier((grad_out, group_tokens, mix_full))
    group_grad_ff = lax.all_gather(grad_out, "tp", axis=0, tiled=True)
    wide = -(-ff // 128) * 128
    pad_wide = lambda a: jnp.pad(a, ((0, wide - ff), (0, 0)))
    ff_pack = jnp.concatenate([pad_wide(jnp.transpose(w_gate)), pad_wide(jnp.transpose(w_up)), pad_wide(w_down)], axis=0)

    taps_all = mix_full[main_w + 2 * heads : proj_w].reshape(spare, fsdp, w_rows)[:, :, :tap_rows]
    taps_all = jnp.transpose(taps_all, (1, 2, 0)).reshape(fsdp, -1)
    cq, cv = conv_query.shape[1], conv_value.shape[1]
    taps_all = taps_all[:, : taps_n * (2 * cq + cv)].reshape(fsdp, taps_n, 2 * cq + cv)
    taps_all = jnp.transpose(taps_all, (1, 0, 2))
    taps = jnp.concatenate(
        [taps_all[:, :, :cq].reshape(taps_n, -1), taps_all[:, :, cq : 2 * cq].reshape(taps_n, -1), taps_all[:, :, 2 * cq :].reshape(taps_n, -1)],
        axis=1,
    ).astype(F32)
    taps = jnp.pad(taps, ((0, 8 - taps_n), (0, 0)))
    log_f, bias_f = decay_log.astype(F32), decay_bias.astype(F32)
    pad_lanes = lambda v: jnp.pad(v, (heads, 128 - 2 * heads))[None, :]
    misc = jnp.pad(jnp.concatenate([pad_lanes(-jnp.exp(log_f)), pad_lanes(bias_f)], axis=0), ((0, 6), (0, 0)))
    gain_row = jnp.tile(head_gain, heads)[None, :]

    group_float = group_tokens.astype(F32)
    mix_scale = norm_scale(group_float)
    normed = (group_float * mix_scale * mix_gain).astype(BF16)
    ff_pack, normed = lax.optimization_barrier((ff_pack, normed))
    proj = lax.dot_general(normed, mix_full[:proj_w], NT, preferred_element_type=F32)
    gated, mixed, u, inverse, start, branch = mixer_fwd(
        proj, taps, misc, gain_row, mix_full, heads, dk, dv, tp, 2, 3)
    branch, group_grad_ff = lax.optimization_barrier((branch, group_grad_ff))
    ff_full = lax.all_gather(ff_pack, "fsdp", axis=1, tiled=True)
    group_state = group_float + branch
    own_rows = lambda full: lax.dynamic_slice_in_dim(full, my_tp * shard_rows, shard_rows, axis=0)
    hidden_state = own_rows(group_state)

    ff_normed, inner, grad_acts, ff_part, ff_gain_grad, sent_sum = feed_forward(
        group_tokens, branch, group_grad_ff, ff_gain[None, :], ff_full, wide, tp, 2, 5)
    ff_gain_grad = ff_gain_grad[0]
    ff_weight_grad = lax.dot_general(ff_normed, grad_acts, TN, preferred_element_type=F32)
    down_grad = lax.dot_general(group_grad_ff, inner, TN, preferred_element_type=F32)
    ff_grads = jnp.concatenate([ff_weight_grad.astype(BF16), down_grad.astype(BF16)], axis=1)
    sent_sum, ff_grads = lax.optimization_barrier((sent_sum, ff_grads))
    ff_sums = lax.psum_scatter(ff_grads, "fsdp", scatter_dimension=0, tiled=True).astype(F32)
    ff_branch = lax.psum_scatter(ff_part, "tp", scatter_dimension=0, tiled=True)
    group_grad_hidden = group_grad_ff.astype(F32) + sent_sum
    group_grad_branch = group_grad_hidden.astype(BF16)
    grad_hidden = own_rows(group_grad_hidden)

    grad_gated = lax.dot_general(group_grad_branch, mix_full[proj_w:], NT, preferred_element_type=F32)
    grad_projected, tap_grads, small, head_gain_grad = mixer_bwd(
        grad_gated, proj, taps, misc, gain_row, mixed, u, inverse, start, heads, dk, dv
    )
    head_part = jnp.sum(head_gain_grad[0].reshape(heads, dv), axis=0)
    decays = jnp.pad(jnp.concatenate([small[0, : 2 * heads], small[1, : 2 * heads]]), (0, 128 - 4 * heads))
    decays = jnp.where(jnp.arange(tp)[:, None] == my_tp, decays[None, :], 0.0).reshape(-1)
    others = jnp.pad(jnp.concatenate([head_part, decays]), (0, d_model - dv - tp * 128))
    small_rows = jnp.pad(jnp.stack([ff_gain_grad, others]), ((1, 5), (0, 0)))
    layer_out = jnp.where(live[:, None], hidden_state + ff_branch.astype(F32), 0.0).astype(BF16)
    input_grad, small_sums, tap_sums, mix_sums = last_sums(
        grad_projected, mix_full, jnp.transpose(normed), group_tokens, mix_gain[None, :], jnp.transpose(group_grad_branch), gated,
        grad_hidden, small_rows, tap_grads, fsdp, tp, 8, 2, 8)
    place = my_tp * fsdp + my_fsdp
    at = lambda row, start, n: lax.dynamic_slice(small_sums, (row, start), (1, n))[0]
    gain_mix_grad = at(0, place * n_mix, n_mix)
    gain_ff_grad = at(1, place * n_mix, n_mix)
    gain_head_grad = at(2, place * n_head, n_head)
    decay_sums = at(2, dv + my_tp * 128, 128)
    tap_at = lambda start, n: lax.dynamic_slice(tap_sums, (0, start + my_fsdp * n), (taps_n, n))
    return (
        layer_out,
        input_grad,
        gain_mix_grad,
        mix_sums[:, :kw],
        mix_sums[:, kw : 2 * kw],
        mix_sums[:, 2 * kw : conv_w],
        mix_sums[:, conv_w:main_w],
        mix_sums[:, main_w : main_w + heads],
        mix_sums[:, main_w + heads : main_w + 2 * heads],
        tap_at(0, cq),
        tap_at(kw, cq),
        tap_at(2 * kw, cv),
        decay_sums[heads : 2 * heads],
        decay_sums[3 * heads : 4 * heads],
        gain_head_grad,
        jnp.transpose(mix_sums[:, proj_w:]),
        gain_ff_grad,
        ff_sums[:, :ff],
        ff_sums[:, wide : wide + ff],
        jnp.transpose(ff_sums[:, 2 * wide : 2 * wide + ff]),
    )


def solution(mesh):
    placed = (
        P(("fsdp", "tp"), None),
        P("fsdp"),
        P(("tp", "fsdp")),
        P("fsdp", "tp"),
        P("fsdp", "tp"),
        P("fsdp", "tp"),
        P("fsdp", "tp"),
        P("fsdp", "tp"),
        P("fsdp", "tp"),
        P(None, ("tp", "fsdp")),
        P(None, ("tp", "fsdp")),
        P(None, ("tp", "fsdp")),
        P("tp"),
        P("tp"),
        P(("tp", "fsdp")),
        P("tp", "fsdp"),
        P(("tp", "fsdp")),
        P("fsdp", "tp"),
        P("fsdp", "tp"),
        P("tp", "fsdp"),
        P(("fsdp", "tp"), None),
    )
    return jax.shard_map(
        body,
        mesh=mesh,
        in_specs=placed,
        out_specs=(
            P(("fsdp", "tp"), None),
            P(("fsdp", "tp"), None),
            P(("tp", "fsdp")),
            P("fsdp", "tp"),
            P("fsdp", "tp"),
            P("fsdp", "tp"),
            P("fsdp", "tp"),
            P("fsdp", "tp"),
            P("fsdp", "tp"),
            P(None, ("tp", "fsdp")),
            P(None, ("tp", "fsdp")),
            P(None, ("tp", "fsdp")),
            P("tp"),
            P("tp"),
            P(("tp", "fsdp")),
            P("tp", "fsdp"),
            P(("tp", "fsdp")),
            P("fsdp", "tp"),
            P("fsdp", "tp"),
            P("tp", "fsdp"),
        ),
        check_vma=False,
    )
```

```python
import functools
import jax
import jax.numpy as jnp
from jax import lax
from jax.experimental import pallas as pl
from jax.experimental.pallas import tpu as pltpu
from jax.sharding import PartitionSpec as P

epsilon = 1e-06
CHUNK = 128
F32 = jnp.float32
BF16 = jnp.bfloat16
NN = (((1,), (0,)), ((), ()))
NT = (((1,), (1,)), ((), ()))
TN = (((0,), (0,)), ((), ()))


def mm(left, right, dims=NN):
    return lax.dot_general(left.astype(BF16), right.astype(BF16), dims, preferred_element_type=F32)


def mm_exact(left, right, dims=NN):
    return lax.dot_general(left, right, dims, precision=lax.Precision.HIGHEST, preferred_element_type=F32)


def sigmoid(x):
    return 1.0 / (1.0 + jnp.exp(-x))


def softplus(x):
    return jnp.maximum(x, 0.0) + jnp.log1p(jnp.exp(-jnp.abs(x)))


def grid_index(shape, axis):
    return lax.broadcasted_iota(jnp.int32, shape, axis)


def unit_inverse(system):
    size = system.shape[0]
    row = grid_index(system.shape, 0)
    col = grid_index(system.shape, 1)
    near = (row // 2) == (col // 2)
    result = jnp.where(row == col, 1.0, 0.0) - jnp.where(near, system, 0.0)
    width = 2
    while width < size:
        joined = (row // (2 * width)) == (col // (2 * width))
        apart = (row // width) != (col // width)
        off = jnp.where(joined & apart, system, 0.0)
        result = result - mm(mm(result, off), result)
        width *= 2
    return result


def rows_ext(ext_ref, offset, rows):
    return ext_ref[pl.ds(offset, rows), :]


def conv_rows(ext_ref, taps_ref, rows):
    total = taps_ref[0:1, :] * ext_ref[pl.ds(8, rows), :]
    for offset in range(1, 4):
        total = total + taps_ref[offset : offset + 1, :] * ext_ref[pl.ds(8 - offset, rows), :]
    return total


def unit_rows(values, scale):
    factor = lax.rsqrt(jnp.sum(values * values, axis=-1, keepdims=True) + epsilon)
    return values * factor * scale, factor


def logits_act(logits, misc_ref, heads):
    lane = grid_index(logits.shape, 1)
    decay = misc_ref[0:1, :] * softplus(logits + misc_ref[1:2, :])
    return jnp.where(lane < heads, sigmoid(logits), decay)


def decay_tables(act, heads):
    rows = act.shape[0]
    row = grid_index((rows, rows), 0)
    col = grid_index((rows, rows), 1)
    tri = jnp.where(row >= col, 1.0, 0.0)
    total = mm_exact(tri, act)
    return total, jnp.transpose(total)


MESH = pl.DeviceIdType.MESH


def cost(micros):
    return pl.CostEstimate(flops=0, bytes_accessed=micros * 3000000, transcendentals=0)


def line_barrier(me, size):
    barrier = pltpu.get_barrier_semaphore()

    @pl.when(me > 0)
    def _():
        pl.semaphore_signal(barrier, inc=1, device_id={"tp": me - 1}, device_id_type=MESH)

    @pl.when(me < size - 1)
    def _():
        pl.semaphore_signal(barrier, inc=1, device_id={"tp": me + 1}, device_id_type=MESH)

    pl.semaphore_wait(barrier, jnp.where(me > 0, 1, 0) + jnp.where(me < size - 1, 1, 0))


PIECE = 32


class StreamSum:
    def __init__(self, size, lag, blocks, x_ref, sum_ref, from_left, from_right, to_left, to_right, sl, sr, rl, rr):
        self.size, self.lag, self.blocks = size, lag, blocks
        self.me = lax.axis_index("tp")
        self.x, self.sum = x_ref, sum_ref
        self.from_left, self.from_right, self.to_left, self.to_right = from_left, from_right, to_left, to_right
        self.sl, self.sr, self.rl, self.rr = sl, sr, rl, rr
        self.half = CHUNK // 2 // PIECE
        self.halves = x_ref.shape[0] // (CHUNK // 2)

    def part(self, ref, p):
        return ref.at[pl.ds(pl.multiple_of(p * PIECE, PIECE), PIECE), :]

    def right(self, src, p):
        return pltpu.make_async_remote_copy(
            src_ref=self.part(src, p), dst_ref=self.part(self.from_left, p), send_sem=self.sr.at[p], recv_sem=self.rl.at[p],
            device_id={"tp": jnp.minimum(self.me + 1, self.size - 1)}, device_id_type=MESH)

    def left(self, src, p):
        return pltpu.make_async_remote_copy(
            src_ref=self.part(src, p), dst_ref=self.part(self.from_right, p), send_sem=self.sl.at[p], recv_sem=self.rr.at[p],
            device_id={"tp": jnp.maximum(self.me - 1, 0)}, device_id_type=MESH)

    def order(self, half):
        return half

    def send_own(self, step):
        @pl.when(self.me == 0)
        def _():
            @pl.loop(0, 2 * self.half)
            def _(k):
                self.right(self.x, self.order(2 * step) * self.half + k).start()

        @pl.when(self.me == self.size - 1)
        def _():
            @pl.loop(0, 2 * self.half)
            def _(k):
                self.left(self.x, self.order(2 * step) * self.half + k).start()

    def advance(self, tick):
        me, size, halves = self.me, self.size, self.halves
        hr = tick - 1 - self.lag * me
        hl = tick - 1 - self.lag * (size - 1 - me)
        hf = tick - 1 - self.lag * jnp.maximum(me, size - 1 - me)

        @pl.loop(0, self.half)
        def _(k):
            @pl.when((me > 0) & (hr >= 0) & (hr < halves))
            def _():
                p = hr * self.half + k
                self.right(self.to_right, p).wait_recv()

                @pl.when(me < size - 1)
                def _():
                    self.part(self.to_right, p)[...] = (
                        self.part(self.from_left, p)[...].astype(F32) + self.part(self.x, p)[...].astype(F32)).astype(BF16)
                    self.right(self.to_right, p).start()

            @pl.when((me < size - 1) & (hl >= 0) & (hl < halves))
            def _():
                p = hl * self.half + k
                self.left(self.to_left, p).wait_recv()

                @pl.when(me > 0)
                def _():
                    self.part(self.to_left, p)[...] = (
                        self.part(self.from_right, p)[...].astype(F32) + self.part(self.x, p)[...].astype(F32)).astype(BF16)
                    self.left(self.to_left, p).start()

            @pl.when((hf >= 0) & (hf < halves))
            def _():
                p = hf * self.half + k
                own = self.part(self.x, p)[...].astype(F32)

                @pl.when(me == 0)
                def _():
                    self.part(self.sum, p)[...] = own + self.part(self.from_right, p)[...].astype(F32)

                @pl.when(me == size - 1)
                def _():
                    self.part(self.sum, p)[...] = own + self.part(self.from_left, p)[...].astype(F32)

                @pl.when((me > 0) & (me < size - 1))
                def _():
                    self.part(self.sum, p)[...] = (
                        own + self.part(self.from_left, p)[...].astype(F32) + self.part(self.from_right, p)[...].astype(F32))

    def finish(self, step):
        @pl.when(step == self.blocks - 1)
        def _():
            @pl.loop(self.halves, self.halves + 1 + self.lag * (self.size - 1))
            def _(tick):
                self.advance(tick)

            @pl.loop(0, self.halves * self.half)
            def _(p):
                @pl.when(self.me < self.size - 1)
                def _():
                    self.right(self.to_right, p).wait_send()

                @pl.when(self.me > 0)
                def _():
                    self.left(self.to_left, p).wait_send()


class StreamGather:
    def __init__(self, size, pieces, x_ref, out_ref, own_sem, sl, sr, rl, rr):
        self.size, self.pieces = size, pieces
        self.me = lax.axis_index("tp")
        self.x, self.out, self.own_sem = x_ref, out_ref, own_sem
        self.sl, self.sr, self.rl, self.rr = sl, sr, rl, rr
        self.shard = x_ref.shape[0]
        self.rows = self.shard // pieces

    def region(self, s, k):
        return self.out.at[pl.ds(pl.multiple_of(s * self.shard + k * self.rows, self.rows), self.rows), :]

    def to_right(self, src, s, k):
        return pltpu.make_async_remote_copy(
            src_ref=src, dst_ref=self.region(s, k), send_sem=self.sr.at[s * self.pieces + k], recv_sem=self.rl.at[s * self.pieces + k],
            device_id={"tp": jnp.minimum(self.me + 1, self.size - 1)}, device_id_type=MESH)

    def to_left(self, src, s, k):
        return pltpu.make_async_remote_copy(
            src_ref=src, dst_ref=self.region(s, k), send_sem=self.sl.at[s * self.pieces + k], recv_sem=self.rr.at[s * self.pieces + k],
            device_id={"tp": jnp.maximum(self.me - 1, 0)}, device_id_type=MESH)

    def own(self):
        here = pl.ds(pl.multiple_of(self.me * self.shard, self.shard), self.shard)
        return pltpu.make_async_copy(self.x, self.out.at[here, :], self.own_sem)

    def start(self):
        self.own().start()
        for k in range(self.pieces):
            src = self.x.at[pl.ds(k * self.rows, self.rows), :]

            @pl.when(self.me < self.size - 1)
            def _():
                self.to_right(src, self.me, k).start()

            @pl.when(self.me > 0)
            def _():
                self.to_left(src, self.me, k).start()

    def tick(self, t):
        d = t // self.pieces + 1
        k = t % self.pieces
        s_left, s_right = self.me - d, self.me + d

        @pl.when((t >= 0) & (d < self.size) & (s_left >= 0))
        def _():
            self.to_right(self.region(s_left, k), s_left, k).wait_recv()

            @pl.when(self.me < self.size - 1)
            def _():
                self.to_right(self.region(s_left, k), s_left, k).start()

        @pl.when((t >= 0) & (d < self.size) & (s_right < self.size))
        def _():
            self.to_left(self.region(s_right, k), s_right, k).wait_recv()

            @pl.when(self.me > 0)
            def _():
                self.to_left(self.region(s_right, k), s_right, k).start()

    def finish(self, steps):
        @pl.loop(steps - 1, max((self.size - 1) * self.pieces, steps - 1))
        def _(t):
            self.tick(t)

        self.own().wait()

        @pl.loop(0, self.size * self.pieces)
        def _(t):
            s, k = t // self.pieces, t % self.pieces

            @pl.when((self.me < self.size - 1) & (s <= self.me))
            def _():
                self.to_right(self.region(s, k), s, k).wait_send()

            @pl.when((self.me > 0) & (s >= self.me))
            def _():
                self.to_left(self.region(s, k), s, k).wait_send()


def stream_scratch(rows, width):
    buf = pltpu.VMEM((rows, width), BF16)
    dma = pltpu.SemaphoreType.DMA((rows // PIECE,))
    return [buf, buf, buf, buf, buf, dma, dma, dma, dma]


def fwd_kernel(
    size, lag, heads, dk, dv, tokens_ref, norm_gain_ref, taps_ref, misc_ref, gain_ref, out_w_ref, shard_ref,
    normed_ref, proj_ref, gated_ref, mixed_ref, u_ref, inv_ref, start_ref, sum_ref, whole_ref, landed, own_sem, gsl, gsr, grl, grr, ext_ref, state_ref, x_ref, *line_refs
):
    rows = CHUNK
    step = pl.program_id(0)
    line = StreamSum(size, lag, pl.num_programs(0), x_ref, sum_ref, *line_refs)
    gather = StreamGather(size, 2, shard_ref, landed, own_sem, gsl, gsr, grl, grr)
    kw, vw = heads * dk, heads * dv
    conv_w = 2 * kw + vw

    @pl.when(step == 0)
    def _():
        line_barrier(line.me, size)
        gather.start()
        ext_ref[0:8, :] = jnp.zeros((8, conv_w), F32)
        state_ref[...] = jnp.zeros_like(state_ref)

    values = tokens_ref[...].astype(F32)
    normed = (values * lax.rsqrt(jnp.mean(values * values, axis=-1, keepdims=True) + epsilon) * norm_gain_ref[...]).astype(BF16)
    normed_ref[...] = normed
    proj_ref[...] = mm(normed, out_w_ref[0 : conv_w + vw + 128, :], NT)
    ext_ref[pl.ds(8, rows), :] = proj_ref[:, 0:conv_w]
    conv = conv_rows(ext_ref, taps_ref, rows)
    ext_ref[0:8, :] = ext_ref[pl.ds(rows, 8), :]
    act = conv * sigmoid(conv)
    logits = logits_act(proj_ref[:, conv_w + vw :], misc_ref, heads)
    cum, cum_t = decay_tables(logits, heads)
    row = grid_index((rows, rows), 0)
    col = grid_index((rows, rows), 1)
    for h in range(heads):
        q, _ = unit_rows(act[:, h * dk : (h + 1) * dk], dk ** (-0.5))
        k, _ = unit_rows(act[:, kw + h * dk : kw + (h + 1) * dk], 1.0)
        v = act[:, 2 * kw + h * dv : 2 * kw + (h + 1) * dv].astype(BF16).astype(F32)
        q, k = q.astype(BF16), k.astype(BF16)
        beta = logits[:, h : h + 1]
        g_col = cum[:, heads + h : heads + h + 1]
        g_row = cum_t[heads + h : heads + h + 1, :]
        decay = jnp.where(row >= col, jnp.exp(jnp.where(row >= col, g_col - g_row, 0.0)), 0.0)
        grams = mm(jnp.concatenate([k, q], axis=0), k, NT)
        system = jnp.where(row > col, decay * grams[:rows], 0.0) * beta
        scores = decay * grams[rows:]
        inverse = unit_inverse(system)
        growth = jnp.exp(g_col)
        g_last = g_row[:, rows - 1 : rows]
        tail = jnp.exp(g_last - g_col)
        state = state_ref[:, h * dv : (h + 1) * dv]
        start_ref[0, :, h * dv : (h + 1) * dv] = state.astype(start_ref.dtype)
        seen = mm(jnp.concatenate([k, q], axis=0), state)
        u = mm(inverse, beta * (v - growth * seen[:rows]))
        mixed = growth * seen[rows:] + mm(scores, u)
        state_ref[:, h * dv : (h + 1) * dv] = jnp.exp(g_last) * state + mm(k, tail * u, TN)
        cols = slice(h * dv, (h + 1) * dv)
        mixed_ref[:, cols] = mixed
        u_ref[:, cols] = u.astype(u_ref.dtype)
        inv_ref[:, h * rows : (h + 1) * rows] = inverse.astype(inv_ref.dtype)
        gate = proj_ref[:, conv_w + h * dv : conv_w + (h + 1) * dv]
        scale = lax.rsqrt(jnp.mean(mixed * mixed, axis=-1, keepdims=True) + epsilon)
        gated = (mixed * scale * gain_ref[:, cols] * gate * sigmoid(gate)).astype(BF16)
        gated_ref[:, cols] = gated
        part = mm(gated, out_w_ref[conv_w + vw + 128 + h * dv : conv_w + vw + 128 + (h + 1) * dv, :])
        branch = part if h == 0 else branch + part
        if h == 0:
            line.advance(2 * step)
    gather.tick(step - 1)
    x_ref[pl.ds(pl.multiple_of(step * rows, rows), rows), :] = branch.astype(BF16)
    line.send_own(step)
    line.advance(2 * step + 1)
    line.finish(step)

    @pl.when(step == pl.num_programs(0) - 1)
    def _():
        gather.finish(total_steps(tokens_ref, sum_ref))
        whole_ref[...] = landed[...]


def total_steps(block_ref, whole_ref):
    return whole_ref.shape[0] // block_ref.shape[0]


def mixer_fwd(tokens, norm_gain, taps, misc, gain, out_w, shard, heads, dk, dv, size, lag, collective_id):
    total_rows = tokens.shape[0]
    chunks = total_rows // CHUNK
    vw = heads * dv
    conv_w = 2 * heads * dk + vw
    model = out_w.shape[1]
    width = conv_w + vw + 128
    blk = lambda w: pl.BlockSpec((CHUNK, w), lambda c: (c, 0))
    full = lambda a: pl.BlockSpec(a.shape, lambda c: (0, 0))
    return pl.pallas_call(
        functools.partial(fwd_kernel, size, lag, heads, dk, dv),
        grid=(chunks,),
        in_specs=[blk(model), full(norm_gain), full(taps), full(misc), full(gain), full(out_w), full(shard)],
        out_specs=[
            blk(model), blk(width), blk(vw), blk(vw), blk(vw), blk(heads * CHUNK), pl.BlockSpec((1, dk, vw), lambda c: (c, 0, 0)),
            pl.BlockSpec((total_rows, model), lambda c: (0, 0)), pl.BlockSpec((total_rows, model), lambda c: (0, 0)),
        ],
        out_shape=[
            jax.ShapeDtypeStruct((total_rows, model), BF16),
            jax.ShapeDtypeStruct((total_rows, width), F32),
            jax.ShapeDtypeStruct((total_rows, vw), BF16),
            jax.ShapeDtypeStruct((total_rows, vw), F32),
            jax.ShapeDtypeStruct((total_rows, vw), BF16),
            jax.ShapeDtypeStruct((total_rows, heads * CHUNK), BF16),
            jax.ShapeDtypeStruct((chunks, dk, vw), BF16),
            jax.ShapeDtypeStruct((total_rows, model), F32),
            jax.ShapeDtypeStruct((total_rows, model), shard.dtype),
        ],
        scratch_shapes=[pltpu.VMEM((total_rows, model), BF16), pltpu.SemaphoreType.DMA] + [pltpu.SemaphoreType.DMA((size * 2,))] * 4
        + [pltpu.VMEM((8 + CHUNK, conv_w), F32), pltpu.VMEM((dk, vw), F32)] + stream_scratch(total_rows, model),
        compiler_params=pltpu.CompilerParams(collective_id=collective_id, has_side_effects=True),
        cost_estimate=cost(88),
        name="mixer_fwd",
    )(tokens, norm_gain, taps, misc, gain, out_w, shard)


def bwd_kernel(heads, dk, dv, out_grad_ref, sent_ref, w_ref, proj_ref, before_ref, taps_ref, misc_ref, gain_ref, mixed_ref, u_ref, inv_ref,
               start_ref, gbranch_ref, gproj_ref, tapg_ref, small_ref, gaing_ref, ext_ref, back_ref, dstate_ref):
    rows = CHUNK
    kw, vw = heads * dk, heads * dv
    conv_w = 2 * kw + vw
    step = pl.program_id(0)
    chunk = pl.num_programs(0) - 1 - step

    @pl.when(step == 0)
    def _():
        back_ref[pl.ds(rows, 8), :] = jnp.zeros((8, conv_w), F32)
        dstate_ref[...] = jnp.zeros_like(dstate_ref)
        tapg_ref[...] = jnp.zeros_like(tapg_ref)
        small_ref[...] = jnp.zeros_like(small_ref)
        gaing_ref[...] = jnp.zeros_like(gaing_ref)

    gbranch = (out_grad_ref[...].astype(F32) + sent_ref[...]).astype(BF16)
    gbranch_ref[...] = gbranch
    grad_gated = mm(gbranch, w_ref[conv_w + vw + 128 :, :], NT)
    ext_ref[0:8, :] = jnp.where(chunk > 0, before_ref[:, 0:conv_w], 0.0)
    ext_ref[pl.ds(8, rows), :] = proj_ref[:, 0:conv_w]
    conv = conv_rows(ext_ref, taps_ref, rows)
    sig = sigmoid(conv)
    act = conv * sig
    dact = sig * (1.0 + conv * (1.0 - sig))
    raw = proj_ref[:, conv_w + vw :]
    logits = logits_act(raw, misc_ref, heads)
    cum, cum_t = decay_tables(logits, heads)
    row = grid_index((rows, rows), 0)
    col = grid_index((rows, rows), 1)
    lane = col
    dlog = jnp.zeros((rows, rows), F32)
    for h in range(heads):
        cols = slice(h * dv, (h + 1) * dv)
        gate = proj_ref[:, conv_w + h * dv : conv_w + (h + 1) * dv]
        gsig = sigmoid(gate)
        mixed = mixed_ref[:, cols]
        grad = grad_gated[:, cols]
        gain = gain_ref[:, cols]
        scale = lax.rsqrt(jnp.mean(mixed * mixed, axis=-1, keepdims=True) + epsilon)
        unit = mixed * scale
        weighted = grad * gate * gsig
        gaing_ref[0:1, cols] += jnp.sum(weighted * unit, axis=0, keepdims=True)
        gproj_ref[:, conv_w + h * dv : conv_w + (h + 1) * dv] = (grad * gain * unit * gsig * (1.0 + gate * (1.0 - gsig))).astype(BF16)
        pulled = weighted * gain
        d_out = scale * (pulled - unit * jnp.mean(pulled * unit, axis=-1, keepdims=True))
        qs, ks = slice(h * dk, (h + 1) * dk), slice(kw + h * dk, kw + (h + 1) * dk)
        vs = slice(2 * kw + h * dv, 2 * kw + (h + 1) * dv)
        q_f, q_scale = unit_rows(act[:, qs], dk ** (-0.5))
        k_f, k_scale = unit_rows(act[:, ks], 1.0)
        v = act[:, vs].astype(BF16).astype(F32)
        q, k = q_f.astype(BF16), k_f.astype(BF16)
        q32, k32 = q.astype(F32), k.astype(F32)
        beta = logits[:, h : h + 1]
        g_col = cum[:, heads + h : heads + h + 1]
        g_row = cum_t[heads + h : heads + h + 1, :]
        decay = jnp.where(row >= col, jnp.exp(jnp.where(row >= col, g_col - g_row, 0.0)), 0.0)
        grams = mm(jnp.concatenate([k, q], axis=0), k, NT)
        plain = jnp.where(row > col, decay * grams[:rows], 0.0)
        scores = decay * grams[rows:]
        growth = jnp.exp(g_col)
        g_last = g_row[:, rows - 1 : rows]
        tail = jnp.exp(g_last - g_col)
        inverse = inv_ref[:, h * rows : (h + 1) * rows]
        u = u_ref[:, cols]
        start = start_ref[0, :, cols]
        d_end = dstate_ref[:, cols]
        d_end_b = d_end.astype(BF16)
        d_u = mm(scores, d_out, TN) + tail * mm(k, d_end_b)
        d_rhs = mm(inverse, d_u, TN)
        d_seen = -growth * d_rhs
        g_out = growth * d_out
        both = mm(jnp.concatenate([d_rhs, d_out], axis=0), u, NT)
        d_sys = jnp.where(row > col, -both[:rows], 0.0)
        d_scores = jnp.where(row >= col, both[rows:], 0.0)
        dstate_ref[:, cols] = jnp.exp(g_last) * d_end + mm(jnp.concatenate([k, q], axis=0), jnp.concatenate([beta * d_seen, g_out], axis=0), TN)
        pull = mm(jnp.concatenate([d_seen, g_out], axis=0), start, NT)
        d_k_seen, d_q1 = pull[:rows], pull[rows:]
        d_k_tail = tail * mm(u, d_end_b, NT)
        d_qk = d_scores * decay
        d_gram = d_sys * decay * beta
        d_gram = d_gram + jnp.transpose(d_gram)
        near = mm(jnp.concatenate([d_qk, d_gram], axis=0), k)
        d_q = d_q1 + near[:rows]
        d_k = beta * d_k_seen + d_k_tail + near[rows:] + mm(d_qk, q, TN)
        d_v = beta * d_rhs
        seen_dot = jnp.sum(k32 * d_k_seen, axis=-1, keepdims=True)
        tail_dot = jnp.sum(k32 * d_k_tail, axis=-1, keepdims=True)
        sys_plain = d_sys * plain
        d_beta = jnp.sum(sys_plain, axis=-1, keepdims=True) + jnp.sum(d_rhs * v, axis=-1, keepdims=True) + seen_dot
        mixed_terms = sys_plain * beta + d_scores * scores
        d_cum = (
            jnp.sum(mixed_terms, axis=-1, keepdims=True)
            - jnp.sum(jnp.transpose(mixed_terms), axis=-1, keepdims=True)
            + beta * seen_dot
            - tail_dot
            + jnp.sum(q32 * d_q1, axis=-1, keepdims=True)
        )
        d_last = jnp.sum(tail_dot, axis=0, keepdims=True) + jnp.exp(g_last) * jnp.sum(
            jnp.sum(d_end * start.astype(F32), axis=-1, keepdims=True), axis=0, keepdims=True
        )
        d_cum = d_cum + jnp.where(grid_index((rows, 1), 0) == rows - 1, d_last, 0.0)
        dlog = jnp.where(lane == h, d_beta, jnp.where(lane == heads + h, d_cum, dlog))
        q_hat, k_hat = q_f * dk**0.5, k_f
        d_q = d_q * dk ** (-0.5)
        d_qa = q_scale * (d_q - q_hat * jnp.sum(d_q * q_hat, axis=-1, keepdims=True))
        d_ka = k_scale * (d_k - k_hat * jnp.sum(d_k * k_hat, axis=-1, keepdims=True))
        back_ref[0:rows, qs] = d_qa * dact[:, qs]
        back_ref[0:rows, ks] = d_ka * dact[:, ks]
        back_ref[0:rows, vs] = d_v * dact[:, vs]
    tri = jnp.where(row <= col, 1.0, 0.0)
    d_decay = mm_exact(tri, dlog)
    shifted = sigmoid(raw + misc_ref[1:2, :])
    d_raw = jnp.where(lane < heads, dlog * logits * (1.0 - logits), d_decay * misc_ref[0:1, :] * shifted)
    d_raw = jnp.where(lane < 2 * heads, d_raw, 0.0)
    gproj_ref[:, conv_w + vw :] = d_raw.astype(BF16)
    small_ref[0:1, :] += jnp.sum(d_decay * logits, axis=0, keepdims=True)
    small_ref[1:2, :] += jnp.sum(d_raw, axis=0, keepdims=True)
    here = back_ref[0:rows, :]
    total = taps_ref[0:1, :] * here
    tapg_ref[0:1, :] += jnp.sum(here * ext_ref[pl.ds(8, rows), :], axis=0, keepdims=True)
    for offset in range(1, 4):
        total = total + taps_ref[offset : offset + 1, :] * back_ref[pl.ds(offset, rows), :]
        tapg_ref[offset : offset + 1, :] += jnp.sum(here * ext_ref[pl.ds(8 - offset, rows), :], axis=0, keepdims=True)
    gproj_ref[:, 0:conv_w] = total.astype(BF16)
    back_ref[pl.ds(rows, 8), :] = back_ref[0:8, :]


def mixer_bwd(out_grad, sent, w_rows, proj, taps, misc, gain, mixed, u, inverse, start, heads, dk, dv):
    total_rows, width = proj.shape
    chunks = total_rows // CHUNK
    conv_w = 2 * heads * dk + heads * dv
    vw = heads * dv
    last = chunks - 1
    model = out_grad.shape[1]
    blk = lambda w: pl.BlockSpec((CHUNK, w), lambda c: (last - c, 0))
    full = lambda a: pl.BlockSpec(a.shape, lambda c: (0, 0))
    per = CHUNK // 8
    return pl.pallas_call(
        functools.partial(bwd_kernel, heads, dk, dv),
        grid=(chunks,),
        in_specs=[
            blk(model), blk(model), full(w_rows), blk(width),
            pl.BlockSpec((8, width), lambda c: (jnp.maximum((last - c) * per - 1, 0), 0)),
            full(taps), full(misc), full(gain), blk(vw), blk(vw), blk(heads * CHUNK),
            pl.BlockSpec((1, dk, vw), lambda c: (last - c, 0, 0)),
        ],
        out_specs=[
            blk(model), blk(width),
            pl.BlockSpec((8, conv_w), lambda c: (0, 0)),
            pl.BlockSpec((8, 128), lambda c: (0, 0)),
            pl.BlockSpec((8, vw), lambda c: (0, 0)),
        ],
        out_shape=[
            jax.ShapeDtypeStruct((total_rows, model), BF16),
            jax.ShapeDtypeStruct((total_rows, width), BF16),
            jax.ShapeDtypeStruct((8, conv_w), F32),
            jax.ShapeDtypeStruct((8, 128), F32),
            jax.ShapeDtypeStruct((8, vw), F32),
        ],
        scratch_shapes=[
            pltpu.VMEM((8 + CHUNK, conv_w), F32),
            pltpu.VMEM((CHUNK + 8, conv_w), F32),
            pltpu.VMEM((dk, vw), F32),
        ],
        cost_estimate=cost(27),
        name="mixer_bwd",
    )(out_grad, sent, w_rows, proj, proj, taps, misc, gain, mixed, u, inverse, start)


def ff_kernel(
    size, lag, wide, tokens_ref, branch_ref, grad_ref, gain_ref, w_ref, normed_ref, inner_ref, acts_ref, part_ref, gaing_ref, sum_ref, x_ref, *line_refs
):
    rows = CHUNK
    step = pl.program_id(0)
    line = StreamSum(size, lag, pl.num_programs(0), x_ref, sum_ref, *line_refs)

    @pl.when(step == 0)
    def _():
        line_barrier(line.me, size)
        gaing_ref[...] = jnp.zeros_like(gaing_ref)

    hidden = (tokens_ref[...].astype(F32) + branch_ref[...]).astype(BF16).astype(F32)
    scale = lax.rsqrt(jnp.mean(hidden * hidden, axis=-1, keepdims=True) + epsilon)
    unit = hidden * scale
    normed = (unit * gain_ref[...]).astype(BF16)
    normed_ref[...] = normed
    gate = mm(normed, w_ref[0:wide, :], NT)
    up = mm(normed, w_ref[wide : 2 * wide, :], NT)
    sig = sigmoid(gate)
    inner = (gate * sig * up).astype(BF16)
    inner_ref[...] = inner
    part_ref[...] = mm(inner, w_ref[2 * wide : 3 * wide, :]).astype(BF16)
    line.advance(2 * step)
    grad_inner = mm(grad_ref[...], w_ref[2 * wide : 3 * wide, :], NT)
    grad_gate = (grad_inner * up * sig * (1.0 + gate * (1.0 - sig))).astype(BF16)
    grad_up = (grad_inner * gate * sig).astype(BF16)
    acts_ref[:, 0:wide] = grad_gate
    acts_ref[:, wide : 2 * wide] = grad_up
    grad_normed = mm(grad_gate, w_ref[0:wide, :]) + mm(grad_up, w_ref[wide : 2 * wide, :])
    gaing_ref[0:1, :] += jnp.sum(grad_normed * unit, axis=0, keepdims=True)
    pulled = grad_normed * gain_ref[...]
    sent = scale * (pulled - unit * jnp.mean(pulled * unit, axis=-1, keepdims=True))
    x_ref[pl.ds(pl.multiple_of(step * rows, rows), rows), :] = sent.astype(BF16)
    line.send_own(step)
    line.advance(2 * step + 1)
    line.finish(step)


def feed_forward(tokens, branch, grad, gain, w_rows, wide, size, lag, collective_id):
    total_rows, model = tokens.shape
    chunks = total_rows // CHUNK
    blk = lambda w: pl.BlockSpec((CHUNK, w), lambda c: (c, 0))
    full = lambda r, w: pl.BlockSpec((r, w), lambda c: (0, 0))
    return pl.pallas_call(
        functools.partial(ff_kernel, size, lag, wide),
        grid=(chunks,),
        in_specs=[blk(model), blk(model), blk(model), full(1, model), full(3 * wide, model)],
        out_specs=[blk(model), blk(wide), blk(2 * wide), blk(model), full(8, model), full(total_rows, model)],
        out_shape=[
            jax.ShapeDtypeStruct((total_rows, model), BF16),
            jax.ShapeDtypeStruct((total_rows, wide), BF16),
            jax.ShapeDtypeStruct((total_rows, 2 * wide), BF16),
            jax.ShapeDtypeStruct((total_rows, model), BF16),
            jax.ShapeDtypeStruct((8, model), F32),
            jax.ShapeDtypeStruct((total_rows, model), F32),
        ],
        scratch_shapes=stream_scratch(total_rows, model),
        compiler_params=pltpu.CompilerParams(collective_id=collective_id, has_side_effects=True),
        cost_estimate=cost(65),
        name="feed_forward",
    )(tokens, branch, grad, gain, w_rows)


def peer_barrier(fsdp, tp):
    me_f, me_t = lax.axis_index("fsdp"), lax.axis_index("tp")
    barrier = pltpu.get_barrier_semaphore()

    @pl.loop(1, fsdp)
    def _(d):
        pl.semaphore_signal(barrier, inc=1, device_id={"fsdp": (me_f + d) % fsdp}, device_id_type=MESH)

    @pl.loop(1, tp)
    def _(d):
        pl.semaphore_signal(barrier, inc=1, device_id={"tp": (me_t + d) % tp}, device_id_type=MESH)

    pl.semaphore_wait(barrier, fsdp + tp - 2)


def line_gather_kernel(fsdp, size, pieces, x_ref, tile_ref, out_ref, tiles_ref, own_sem, sl, sr, rl, rr, sp, rp, st, rt):
    me = lax.axis_index("tp")
    shard = x_ref.shape[0]
    rows = shard // pieces
    own = pltpu.make_async_copy(x_ref, out_ref.at[pl.ds(pl.multiple_of(me * shard, shard), shard), :], own_sem)
    own.start()
    me_f = lax.axis_index("fsdp")
    tiles_ref[pl.ds(me_f, 1), pl.ds(me, 1)] = tile_ref[...][None, None]
    peer_barrier(fsdp, size)

    def along(d, slot):
        return pltpu.make_async_remote_copy(
            src_ref=tile_ref, dst_ref=tiles_ref.at[me_f, slot], send_sem=st.at[d], recv_sem=rt.at[slot],
            device_id={"tp": (me + d) % size}, device_id_type=MESH)

    def across(d, slot):
        return pltpu.make_async_remote_copy(
            src_ref=tiles_ref.at[me_f], dst_ref=tiles_ref.at[slot], send_sem=sp.at[d], recv_sem=rp.at[slot],
            device_id={"fsdp": (me_f + d) % fsdp}, device_id_type=MESH)

    @pl.loop(1, size)
    def _(d):
        along(d, me).start()

    def region(ref, s, k):
        return ref.at[pl.ds(pl.multiple_of(s * shard + k * rows, rows), rows), :]

    def to_right(src, s, k):
        return pltpu.make_async_remote_copy(
            src_ref=src, dst_ref=region(out_ref, s, k), send_sem=sr.at[s * pieces + k], recv_sem=rl.at[s * pieces + k],
            device_id={"tp": jnp.minimum(me + 1, size - 1)}, device_id_type=MESH)

    def to_left(src, s, k):
        return pltpu.make_async_remote_copy(
            src_ref=src, dst_ref=region(out_ref, s, k), send_sem=sl.at[s * pieces + k], recv_sem=rr.at[s * pieces + k],
            device_id={"tp": jnp.maximum(me - 1, 0)}, device_id_type=MESH)

    for k in range(pieces):
        src = x_ref.at[pl.ds(k * rows, rows), :]

        @pl.when(me < size - 1)
        def _():
            to_right(src, me, k).start()

        @pl.when(me > 0)
        def _():
            to_left(src, me, k).start()

    @pl.loop(1, size)
    def _(d):
        along(d, (me + d) % size).wait_recv()

    @pl.loop(1, fsdp)
    def _(d):
        across(d, me_f).start()

    @pl.loop(0, (size - 1) * pieces)
    def _(t):
        d = t // pieces + 1
        k = t % pieces
        s_left, s_right = me - d, me + d

        @pl.when(s_left >= 0)
        def _():
            to_right(region(out_ref, s_left, k), s_left, k).wait_recv()

            @pl.when(me < size - 1)
            def _():
                to_right(region(out_ref, s_left, k), s_left, k).start()

        @pl.when(s_right < size)
        def _():
            to_left(region(out_ref, s_right, k), s_right, k).wait_recv()

            @pl.when(me > 0)
            def _():
                to_left(region(out_ref, s_right, k), s_right, k).start()

    own.wait()

    @pl.loop(1, fsdp)
    def _(d):
        across(d, (me_f + d) % fsdp).wait_recv()

    @pl.loop(1, size)
    def _(d):
        along(d, me).wait_send()

    @pl.loop(1, fsdp)
    def _(d):
        across(d, me_f).wait_send()

    @pl.loop(0, size * pieces)
    def _(t):
        s, k = t // pieces, t % pieces

        @pl.when((me < size - 1) & (s <= me))
        def _():
            to_right(region(out_ref, s, k), s, k).wait_send()

        @pl.when((me > 0) & (s >= me))
        def _():
            to_left(region(out_ref, s, k), s, k).wait_send()


def line_gather(x, tile, fsdp, size, pieces, collective_id):
    vm = pl.BlockSpec(memory_space=pltpu.VMEM)
    dma = pltpu.SemaphoreType.DMA((size * pieces,))
    plane, line = pltpu.SemaphoreType.DMA((fsdp,)), pltpu.SemaphoreType.DMA((size,))
    return pl.pallas_call(
        functools.partial(line_gather_kernel, fsdp, size, pieces),
        out_shape=[
            jax.ShapeDtypeStruct((size * x.shape[0], x.shape[1]), x.dtype),
            jax.ShapeDtypeStruct((fsdp, size) + tile.shape, tile.dtype),
        ],
        in_specs=[vm, vm], out_specs=[vm, vm],
        scratch_shapes=[pltpu.SemaphoreType.DMA, dma, dma, dma, dma, plane, plane, line, line],
        compiler_params=pltpu.CompilerParams(collective_id=collective_id, has_side_effects=True),
        cost_estimate=cost(40),
        name="line_gather",
    )(x, tile)


class PlaneSum:
    def __init__(self, n, order, cols, src_ref, out_ref, acc_ref, recv_ref, send_sem, recv_sem):
        self.n, self.order, self.cols = n, order, cols
        self.stages = len(order)
        self.me = lax.axis_index("fsdp")
        self.block = src_ref.shape[0] // n
        self.src, self.out, self.acc, self.recv = src_ref, out_ref, acc_ref, recv_ref
        self.send_sem, self.recv_sem = send_sem, recv_sem

    def bit(self, b):
        return (self.me // b) % 2

    def owner(self, stage, i, flip):
        total = 0
        for b in self.order[:stage]:
            total = total + self.bit(b) * b
        b = self.order[stage]
        total = total + ((1 - self.bit(b)) if flip else self.bit(b)) * b
        for j, r in enumerate(self.order[stage + 1 :]):
            total = total + ((i // (2**j)) % 2) * r
        return total

    def place(self, pair):
        total = 0
        for j, r in enumerate(self.order[1:]):
            total = total + ((pair // (r // 2)) % 2) * 2**j
        return total

    def rows(self, g):
        return pl.ds(pl.multiple_of(g * self.block, self.block), self.block)

    def copy(self, stage, i):
        b = self.order[stage]
        src = self.src if stage == 0 else self.acc
        slot = self.n - (self.n >> stage) + i
        return pltpu.make_async_remote_copy(
            src_ref=src.at[self.rows(self.owner(stage, i, True)), self.cols], dst_ref=self.recv.at[self.rows(slot), self.cols],
            send_sem=self.send_sem.at[slot], recv_sem=self.recv_sem.at[slot],
            device_id={"fsdp": self.me + b - 2 * b * self.bit(b)}, device_id_type=MESH)

    def total(self, stage, i):
        self.copy(stage, i).wait_recv()
        g = self.owner(stage, i, False)
        slot = self.n - (self.n >> stage) + i
        src = self.src if stage == 0 else self.acc
        return g, src[self.rows(g), self.cols].astype(F32) + self.recv[self.rows(slot), self.cols].astype(F32)

    def advance(self, stage):
        if stage == self.stages - 1:
            _, total = self.total(stage, 0)
            self.out[:, self.cols] = total
            return
        mine = self.bit(self.order[stage + 1])
        for flip in (True, False):
            @pl.loop(0, self.n >> (stage + 2))
            def _(i):
                g, total = self.total(stage, 2 * i + (1 - mine if flip else mine))
                self.acc[self.rows(g), self.cols] = total.astype(BF16)
                if flip:
                    self.copy(stage + 1, i).start()

    def advance_pair(self, pair):
        i = self.place(pair)
        g, total = self.total(0, i)
        self.acc[self.rows(g), self.cols] = total.astype(BF16)

        @pl.when(i % 2 != self.bit(self.order[1]))
        def _():
            self.copy(1, i // 2).start()

    def finish(self):
        @pl.loop(0, self.n // 2)
        def _(i):
            self.copy(0, i).wait_send()

        for stage in range(1, self.stages):
            @pl.loop(0, self.n >> (stage + 1))
            def _(i):
                self.copy(stage, i).wait_send()


def halving_orders(n):
    bits = [2**j for j in range(n.bit_length() - 1)]
    return bits, bits[:1] + bits[:0:-1]


def last_kernel(
    fsdp, size, pieces, slack, gproj_ref, w_ref, normed_ref, tokens_ref, gain_ref, gbranch_ref, gated_ref, base_ref, small_ref, tapg_ref,
    out_ref, small_out, tap_out, shard_ref,
    x_ref, grads, acc, recv, small, small_in, small_line, tap_in, from_left, from_right, to_left, to_right,
    sl, sr, rl, rr, sp, rp, st, rt, sk, rk, sa, ra, sb, rb
):
    me, me_f = lax.axis_index("tp"), lax.axis_index("fsdp")
    shard = x_ref.shape[0] // size
    rows = shard // pieces
    count = (size - 1) * pieces
    proj_w = gproj_ref.shape[1]
    peer_barrier(fsdp, size)

    def across(d, slot):
        return pltpu.make_async_remote_copy(
            src_ref=small, dst_ref=small_in.at[slot], send_sem=sp.at[d], recv_sem=rp.at[slot],
            device_id={"fsdp": (me_f + d) % fsdp}, device_id_type=MESH)

    def taps_across(d, slot):
        return pltpu.make_async_remote_copy(
            src_ref=tapg_ref, dst_ref=tap_in.at[slot], send_sem=sk.at[d], recv_sem=rk.at[slot],
            device_id={"fsdp": (me_f + d) % fsdp}, device_id_type=MESH)

    def along(d, slot):
        return pltpu.make_async_remote_copy(
            src_ref=small_out, dst_ref=small_line.at[slot], send_sem=st.at[d], recv_sem=rt.at[slot],
            device_id={"tp": (me + d) % size}, device_id_type=MESH)

    width = grads.shape[1]
    cut = (width // 256 + width // 128 % 2) * 128
    order_a, order_b = halving_orders(fsdp)
    planes = [
        PlaneSum(fsdp, order_a, slice(0, cut), grads, shard_ref, acc, recv, sa, ra),
        PlaneSum(fsdp, order_b, slice(cut, width), grads, shard_ref, acc, recv, sb, rb),
    ]

    def part(ref, s, k):
        return ref.at[pl.ds(pl.multiple_of(s * shard + k * rows, rows), rows), :]

    def right_copy(src, s, k):
        return pltpu.make_async_remote_copy(
            src_ref=part(src, s, k), dst_ref=part(from_left, s, k), send_sem=sr.at[s * pieces + k], recv_sem=rl.at[s * pieces + k],
            device_id={"tp": jnp.minimum(me + 1, size - 1)}, device_id_type=MESH)

    def left_copy(src, s, k):
        return pltpu.make_async_remote_copy(
            src_ref=part(src, s, k), dst_ref=part(from_right, s, k), send_sem=sl.at[s * pieces + k], recv_sem=rr.at[s * pieces + k],
            device_id={"tp": jnp.maximum(me - 1, 0)}, device_id_type=MESH)

    def exchange(t):
        ir = t - (me - 1) * slack
        il = t - (size - 2 - me) * slack
        s_r, k_r = size - 1 - ir // pieces, ir % pieces
        s_l, k_l = il // pieces, il % pieces

        @pl.when((me > 0) & (ir >= 0) & (ir < count) & (s_r >= me))
        def _():
            right_copy(to_right, s_r, k_r).wait_recv()

            @pl.when(s_r > me)
            def _():
                part(to_right, s_r, k_r)[...] = (
                    part(from_left, s_r, k_r)[...].astype(F32) + part(x_ref, s_r, k_r)[...].astype(F32)).astype(BF16)
                right_copy(to_right, s_r, k_r).start()

        @pl.when((me < size - 1) & (il >= 0) & (il < count) & (s_l <= me))
        def _():
            left_copy(to_left, s_l, k_l).wait_recv()

            @pl.when(s_l < me)
            def _():
                part(to_left, s_l, k_l)[...] = (
                    part(from_right, s_l, k_l)[...].astype(F32) + part(x_ref, s_l, k_l)[...].astype(F32)).astype(BF16)
                left_copy(to_left, s_l, k_l).start()

    small[...] = small_ref[...]

    @pl.loop(0, size)
    def _(j):
        s = (j % 2) * (j // 2) + (1 - j % 2) * (size - 1 - j // 2)
        here = pl.ds(pl.multiple_of(s * shard, shard), shard)
        grad_normed = mm(gproj_ref[here, :], w_ref[0:proj_w, :])
        values = tokens_ref[here, :].astype(F32)
        scale = lax.rsqrt(jnp.mean(values * values, axis=-1, keepdims=True) + epsilon)
        unit = values * scale
        small[0:1, :] += jnp.sum(grad_normed * unit, axis=0, keepdims=True)
        pulled = grad_normed * gain_ref[...]
        x_ref[here, :] = (scale * (pulled - unit * jnp.mean(pulled * unit, axis=-1, keepdims=True))).astype(BF16)

        @pl.when((me == 0) & (s > 0))
        def _():
            @pl.loop(0, pieces)
            def _(k):
                right_copy(x_ref, s, k).start()

        @pl.when((me == size - 1) & (s < size - 1))
        def _():
            @pl.loop(0, pieces)
            def _(k):
                left_copy(x_ref, s, k).start()

    @pl.loop(1, fsdp)
    def _(d):
        taps_across(d, me_f).start()
        across(d, me_f).start()

    block = grads.shape[0] // fsdp
    many = max(256 // block, 2)
    groups = fsdp // many
    ticks = count + (size - 2) * slack
    per = max(3 * ticks // (7 * groups), 1)
    pairs = many // 2

    def group_at(i):
        mine, other = me_f // many, groups - 1 - i
        total = 0
        for b in halving_orders(groups)[0]:
            total = total + ((mine // b + other // b) % 2) * b
        return total

    def advance_group(i):
        @pl.loop(0, pairs)
        def _(m):
            for plane in planes:
                plane.advance_pair(group_at(i) * pairs + m)

    @pl.loop(0, groups)
    def _(i):
        g = group_at(i)
        here = pl.ds(pl.multiple_of(g * many * block, many * block), many * block)
        grads[here, 0:proj_w] = mm(normed_ref[:, here], gproj_ref[...], TN).astype(BF16)
        grads[here, proj_w:width] = mm(gbranch_ref[:, here], gated_ref[...], TN).astype(BF16)

        @pl.loop(0, pairs)
        def _(m):
            for plane in planes:
                plane.copy(0, plane.place(g * pairs + m)).start()

        @pl.loop(i * per, (i + 1) * per)
        def _(t):
            exchange(t)

        @pl.when(i > 0)
        def _():
            advance_group(i - 1)

    advance_group(groups - 1)
    stages = len(order_a)
    done = groups * per
    for stage in range(stages):
        if stage > 0:
            until = max(done, int(ticks * (0.68 + 0.24 * (stage - 1) / max(stages - 2, 1))))

            @pl.loop(done, until)
            def _(t):
                exchange(t)

            done = until
            for plane in planes:
                plane.advance(stage)
        if stage == 0:
            small_out[...] = small[...]
            tap_out[...] = tapg_ref[...]

            @pl.loop(1, fsdp)
            def _(d):
                slot = (me_f + d) % fsdp
                across(d, slot).wait_recv()
                taps_across(d, slot).wait_recv()
                small_out[...] += small_in[pl.ds(slot, 1)][0]
                tap_out[...] += tap_in[pl.ds(slot, 1)][0]

            @pl.loop(1, size)
            def _(d):
                along(d, me).start()

    @pl.loop(done, ticks)
    def _(t):
        exchange(t)

    for plane in planes:
        plane.finish()

    @pl.loop(1, size)
    def _(d):
        along(d, me).wait_send()

    @pl.loop(1, size)
    def _(d):
        slot = (me + d) % size
        along(d, slot).wait_recv()
        small_out[...] += small_line[pl.ds(slot, 1)][0]

    @pl.loop(1, fsdp)
    def _(d):
        across(d, me_f).wait_send()
        taps_across(d, me_f).wait_send()

    @pl.loop(0, pieces)
    def _(k):
        here = pl.ds(pl.multiple_of(k * rows, rows), rows)
        total = base_ref[here, :] + part(x_ref, me, k)[...].astype(F32)

        @pl.when(me == 0)
        def _():
            out_ref[here, :] = total + part(from_right, me, k)[...].astype(F32)

        @pl.when(me == size - 1)
        def _():
            out_ref[here, :] = total + part(from_left, me, k)[...].astype(F32)

        @pl.when((me > 0) & (me < size - 1))
        def _():
            out_ref[here, :] = total + part(from_left, me, k)[...].astype(F32) + part(from_right, me, k)[...].astype(F32)

    @pl.loop(0, size * pieces)
    def _(i):
        s, k = i // pieces, i % pieces

        @pl.when(s > me)
        def _():
            right_copy(to_right, s, k).wait_send()

        @pl.when(s < me)
        def _():
            left_copy(to_left, s, k).wait_send()


def last_sums(gproj, w_rows, normed, tokens, gain, gbranch, gated, base, small, tapg, fsdp, size, pieces, slack, collective_id):
    vm = pl.BlockSpec(memory_space=pltpu.VMEM)
    total_rows, model = tokens.shape
    width = gproj.shape[1] + gated.shape[1]
    buf = pltpu.VMEM((total_rows, model), BF16)
    pack = pltpu.VMEM((model, width), BF16)
    dma = pltpu.SemaphoreType.DMA((size * pieces,))
    plane, line = pltpu.SemaphoreType.DMA((fsdp,)), pltpu.SemaphoreType.DMA((size,))
    return pl.pallas_call(
        functools.partial(last_kernel, fsdp, size, pieces, slack),
        out_shape=[
            jax.ShapeDtypeStruct(base.shape, F32), jax.ShapeDtypeStruct(small.shape, F32), jax.ShapeDtypeStruct(tapg.shape, F32),
            jax.ShapeDtypeStruct((model // fsdp, width), F32),
        ],
        in_specs=[vm] * 10, out_specs=[vm] * 4,
        scratch_shapes=[
            buf, pack, pack, pack, pltpu.VMEM(small.shape, F32), pltpu.VMEM((fsdp,) + small.shape, F32), pltpu.VMEM((size,) + small.shape, F32),
            pltpu.VMEM((fsdp,) + tapg.shape, F32), buf, buf, buf, buf,
            dma, dma, dma, dma, plane, plane, line, line, plane, plane, plane, plane, plane, plane,
        ],
        compiler_params=pltpu.CompilerParams(collective_id=collective_id, has_side_effects=True),
        cost_estimate=cost(55),
        name="last_sums",
    )(gproj, w_rows, normed, tokens, gain, gbranch, gated, base, small, tapg)


def norm_scale(values):
    return lax.rsqrt(jnp.mean(values * values, axis=-1, keepdims=True) + epsilon)


def norm_back(grad_normed, values, scale, gain):
    unit = values * scale
    gain_grad = jnp.sum(grad_normed * unit, axis=0)
    pulled = grad_normed * gain
    input_part = scale * (pulled - unit * jnp.mean(pulled * unit, axis=-1, keepdims=True))
    return (input_part, gain_grad)


def body(
    tokens, lengths, gain_mix, w_query, w_key, w_value, w_outgate, w_beta, w_decay,
    conv_query, conv_key, conv_value, decay_log, decay_bias, gain_head, w_out, gain_ff,
    w_gate, w_up, w_down, cotangent,
):
    fsdp, tp = lax.axis_size("fsdp"), lax.axis_size("tp")
    my_fsdp, my_tp = lax.axis_index("fsdp"), lax.axis_index("tp")
    shard_rows, d_model = tokens.shape
    w_rows = w_query.shape[0]
    heads = w_beta.shape[1]
    kw, vw = w_query.shape[1], w_value.shape[1]
    dk, dv = kw // heads, vw // heads
    conv_w = 2 * kw + vw
    main_w = conv_w + vw
    proj_w = main_w + 128
    ff = w_gate.shape[1]
    taps_n = conv_query.shape[0]

    taps_local = jnp.concatenate([conv_query, conv_key, conv_value], axis=1).reshape(1, -1)
    spare = 128 - 2 * heads
    tap_rows = -(-taps_local.shape[1] // spare)
    taps_pack = jnp.pad(taps_local, ((0, 0), (0, tap_rows * spare - taps_local.shape[1]))).reshape(tap_rows, spare)
    taps_pack = jnp.pad(taps_pack, ((0, w_rows - tap_rows), (0, 0)))
    extras = jnp.concatenate([w_beta, w_decay, taps_pack], axis=1)
    mix_pack = jnp.concatenate([jnp.transpose(a) for a in (w_query, w_key, w_value, w_outgate, extras)] + [w_out], axis=0)
    mix_pack, tokens = lax.optimization_barrier((mix_pack, tokens))
    mix_full = lax.all_gather(mix_pack, "fsdp", axis=1, tiled=True)
    n_mix, n_head = gain_mix.shape[0], gain_head.shape[0]
    gains_local = jnp.concatenate([gain_mix, gain_head, gain_ff]).astype(F32)
    gains_tile = jnp.pad(gains_local[None, :], ((0, 7), (0, 128 - gains_local.shape[0])))
    group_tokens, gains = line_gather(tokens, gains_tile, fsdp, tp, 2, 4)
    gains = jnp.transpose(gains[:, :, 0, :], (1, 0, 2)).reshape(tp * fsdp, 128)
    mix_gain = gains[:, :n_mix].reshape(-1)
    head_gain = gains[:, n_mix : n_mix + n_head].reshape(-1)
    ff_gain = gains[:, n_mix + n_head : 2 * n_mix + n_head].reshape(-1)
    live = my_tp * shard_rows + jnp.arange(shard_rows, dtype=jnp.int32) < lengths[0]
    grad_out = jnp.where(live[:, None], cotangent, jnp.zeros_like(cotangent))
    wide = -(-ff // 128) * 128
    pad_wide = lambda a: jnp.pad(a, ((0, wide - ff), (0, 0)))
    ff_pack = jnp.concatenate([pad_wide(jnp.transpose(w_gate)), pad_wide(jnp.transpose(w_up)), pad_wide(w_down)], axis=0)

    taps_all = mix_full[main_w + 2 * heads : proj_w].reshape(spare, fsdp, w_rows)[:, :, :tap_rows]
    taps_all = jnp.transpose(taps_all, (1, 2, 0)).reshape(fsdp, -1)
    cq, cv = conv_query.shape[1], conv_value.shape[1]
    taps_all = taps_all[:, : taps_n * (2 * cq + cv)].reshape(fsdp, taps_n, 2 * cq + cv)
    taps_all = jnp.transpose(taps_all, (1, 0, 2))
    taps = jnp.concatenate(
        [taps_all[:, :, :cq].reshape(taps_n, -1), taps_all[:, :, cq : 2 * cq].reshape(taps_n, -1), taps_all[:, :, 2 * cq :].reshape(taps_n, -1)],
        axis=1,
    ).astype(F32)
    taps = jnp.pad(taps, ((0, 8 - taps_n), (0, 0)))
    log_f, bias_f = decay_log.astype(F32), decay_bias.astype(F32)
    pad_lanes = lambda v: jnp.pad(v, (heads, 128 - 2 * heads))[None, :]
    misc = jnp.pad(jnp.concatenate([pad_lanes(-jnp.exp(log_f)), pad_lanes(bias_f)], axis=0), ((0, 6), (0, 0)))
    gain_row = jnp.tile(head_gain, heads)[None, :]

    normed, proj, gated, mixed, u, inverse, start, branch, group_grad_ff = mixer_fwd(
        group_tokens, mix_gain[None, :], taps, misc, gain_row, mix_full, grad_out, heads, dk, dv, tp, 2, 3)
    ff_full = lax.all_gather(ff_pack, "fsdp", axis=1, tiled=True)
    own_rows = lambda full: lax.dynamic_slice_in_dim(full, my_tp * shard_rows, shard_rows, axis=0)
    hidden_state = tokens.astype(F32) + own_rows(branch)

    ff_normed, inner, grad_acts, ff_part, ff_gain_grad, sent_sum = feed_forward(
        group_tokens, branch, group_grad_ff, ff_gain[None, :], ff_full, wide, tp, 2, 5)
    ff_gain_grad = ff_gain_grad[0]
    ff_weight_grad = lax.dot_general(ff_normed, grad_acts, TN, preferred_element_type=F32)
    down_grad = lax.dot_general(group_grad_ff, inner, TN, preferred_element_type=F32)
    ff_grads = jnp.concatenate([ff_weight_grad.astype(BF16), down_grad.astype(BF16)], axis=1)
    sent_sum, ff_grads = lax.optimization_barrier((sent_sum, ff_grads))
    ff_sums = lax.psum_scatter(ff_grads, "fsdp", scatter_dimension=0, tiled=True).astype(F32)
    ff_branch = lax.psum_scatter(ff_part, "tp", scatter_dimension=0, tiled=True)
    grad_hidden = grad_out.astype(F32) + own_rows(sent_sum)

    group_grad_branch, grad_projected, tap_grads, small, head_gain_grad = mixer_bwd(
        group_grad_ff, sent_sum, mix_full, proj, taps, misc, gain_row, mixed, u, inverse, start, heads, dk, dv
    )
    ff_branch, grad_projected = lax.optimization_barrier((ff_branch, grad_projected))
    head_part = jnp.sum(head_gain_grad[0].reshape(heads, dv), axis=0)
    decays = jnp.pad(jnp.concatenate([small[0, : 2 * heads], small[1, : 2 * heads]]), (0, 128 - 4 * heads))
    decays = jnp.where(jnp.arange(tp)[:, None] == my_tp, decays[None, :], 0.0).reshape(-1)
    others = jnp.pad(jnp.concatenate([head_part, decays]), (0, d_model - dv - tp * 128))
    small_rows = jnp.pad(jnp.stack([ff_gain_grad, others]), ((1, 5), (0, 0)))
    layer_out = jnp.where(live[:, None], hidden_state + ff_branch.astype(F32), 0.0).astype(BF16)
    input_grad, small_sums, tap_sums, mix_sums = last_sums(
        grad_projected, mix_full, normed, group_tokens, mix_gain[None, :], group_grad_branch, gated,
        grad_hidden, small_rows, tap_grads, fsdp, tp, 8, 2, 8)
    place = my_tp * fsdp + my_fsdp
    at = lambda row, start, n: lax.dynamic_slice(small_sums, (row, start), (1, n))[0]
    gain_mix_grad = at(0, place * n_mix, n_mix)
    gain_ff_grad = at(1, place * n_mix, n_mix)
    gain_head_grad = at(2, place * n_head, n_head)
    decay_sums = at(2, dv + my_tp * 128, 128)
    tap_at = lambda start, n: lax.dynamic_slice(tap_sums, (0, start + my_fsdp * n), (taps_n, n))
    return (
        layer_out,
        input_grad,
        gain_mix_grad,
        mix_sums[:, :kw],
        mix_sums[:, kw : 2 * kw],
        mix_sums[:, 2 * kw : conv_w],
        mix_sums[:, conv_w:main_w],
        mix_sums[:, main_w : main_w + heads],
        mix_sums[:, main_w + heads : main_w + 2 * heads],
        tap_at(0, cq),
        tap_at(kw, cq),
        tap_at(2 * kw, cv),
        decay_sums[heads : 2 * heads],
        decay_sums[3 * heads : 4 * heads],
        gain_head_grad,
        jnp.transpose(mix_sums[:, proj_w:]),
        gain_ff_grad,
        ff_sums[:, :ff],
        ff_sums[:, wide : wide + ff],
        jnp.transpose(ff_sums[:, 2 * wide : 2 * wide + ff]),
    )


def solution(mesh):
    placed = (
        P(("fsdp", "tp"), None),
        P("fsdp"),
        P(("tp", "fsdp")),
        P("fsdp", "tp"),
        P("fsdp", "tp"),
        P("fsdp", "tp"),
        P("fsdp", "tp"),
        P("fsdp", "tp"),
        P("fsdp", "tp"),
        P(None, ("tp", "fsdp")),
        P(None, ("tp", "fsdp")),
        P(None, ("tp", "fsdp")),
        P("tp"),
        P("tp"),
        P(("tp", "fsdp")),
        P("tp", "fsdp"),
        P(("tp", "fsdp")),
        P("fsdp", "tp"),
        P("fsdp", "tp"),
        P("tp", "fsdp"),
        P(("fsdp", "tp"), None),
    )
    return jax.shard_map(
        body,
        mesh=mesh,
        in_specs=placed,
        out_specs=(
            P(("fsdp", "tp"), None),
            P(("fsdp", "tp"), None),
            P(("tp", "fsdp")),
            P("fsdp", "tp"),
            P("fsdp", "tp"),
            P("fsdp", "tp"),
            P("fsdp", "tp"),
            P("fsdp", "tp"),
            P("fsdp", "tp"),
            P(None, ("tp", "fsdp")),
            P(None, ("tp", "fsdp")),
            P(None, ("tp", "fsdp")),
            P("tp"),
            P("tp"),
            P(("tp", "fsdp")),
            P("tp", "fsdp"),
            P(("tp", "fsdp")),
            P("fsdp", "tp"),
            P("fsdp", "tp"),
            P("tp", "fsdp"),
        ),
        check_vma=False,
    )
```

```python
import functools
import jax
import jax.numpy as jnp
from jax import lax
from jax.experimental import pallas as pl
from jax.experimental.pallas import tpu as pltpu
from jax.sharding import PartitionSpec as P

epsilon = 1e-06
CHUNK = 128
F32 = jnp.float32
BF16 = jnp.bfloat16
NN = (((1,), (0,)), ((), ()))
NT = (((1,), (1,)), ((), ()))
TN = (((0,), (0,)), ((), ()))


def mm(left, right, dims=NN):
    return lax.dot_general(left.astype(BF16), right.astype(BF16), dims, preferred_element_type=F32)


def mm_exact(left, right, dims=NN):
    return lax.dot_general(left, right, dims, precision=lax.Precision.HIGHEST, preferred_element_type=F32)


def sigmoid(x):
    return 1.0 / (1.0 + jnp.exp(-x))


def softplus(x):
    return jnp.maximum(x, 0.0) + jnp.log1p(jnp.exp(-jnp.abs(x)))


def grid_index(shape, axis):
    return lax.broadcasted_iota(jnp.int32, shape, axis)


def unit_inverse(system):
    size = system.shape[0]
    row = grid_index(system.shape, 0)
    col = grid_index(system.shape, 1)
    near = (row // 2) == (col // 2)
    result = jnp.where(row == col, 1.0, 0.0) - jnp.where(near, system, 0.0)
    width = 2
    while width < size:
        joined = (row // (2 * width)) == (col // (2 * width))
        apart = (row // width) != (col // width)
        off = jnp.where(joined & apart, system, 0.0)
        result = result - mm(mm(result, off), result)
        width *= 2
    return result


def rows_ext(ext_ref, offset, rows):
    return ext_ref[pl.ds(offset, rows), :]


def conv_rows(ext_ref, taps_ref, rows):
    total = taps_ref[0:1, :] * ext_ref[pl.ds(8, rows), :]
    for offset in range(1, 4):
        total = total + taps_ref[offset : offset + 1, :] * ext_ref[pl.ds(8 - offset, rows), :]
    return total


def unit_rows(values, scale):
    factor = lax.rsqrt(jnp.sum(values * values, axis=-1, keepdims=True) + epsilon)
    return values * factor * scale, factor


def logits_act(logits, misc_ref, heads):
    lane = grid_index(logits.shape, 1)
    decay = misc_ref[0:1, :] * softplus(logits + misc_ref[1:2, :])
    return jnp.where(lane < heads, sigmoid(logits), decay)


def decay_tables(act, heads):
    rows = act.shape[0]
    row = grid_index((rows, rows), 0)
    col = grid_index((rows, rows), 1)
    tri = jnp.where(row >= col, 1.0, 0.0)
    total = mm_exact(tri, act)
    return total, jnp.transpose(total)


MESH = pl.DeviceIdType.MESH


def cost(micros):
    return pl.CostEstimate(flops=0, bytes_accessed=micros * 3000000, transcendentals=0)


def line_barrier(me, size):
    barrier = pltpu.get_barrier_semaphore()

    @pl.when(me > 0)
    def _():
        pl.semaphore_signal(barrier, inc=1, device_id={"tp": me - 1}, device_id_type=MESH)

    @pl.when(me < size - 1)
    def _():
        pl.semaphore_signal(barrier, inc=1, device_id={"tp": me + 1}, device_id_type=MESH)

    pl.semaphore_wait(barrier, jnp.where(me > 0, 1, 0) + jnp.where(me < size - 1, 1, 0))


PIECE = 64


class StreamSum:
    def __init__(self, size, lag, blocks, x_ref, sum_ref, from_left, from_right, to_left, to_right, sl, sr, rl, rr):
        self.size, self.lag, self.blocks = size, lag, blocks
        self.me = lax.axis_index("tp")
        self.x, self.sum = x_ref, sum_ref
        self.from_left, self.from_right, self.to_left, self.to_right = from_left, from_right, to_left, to_right
        self.sl, self.sr, self.rl, self.rr = sl, sr, rl, rr
        self.half = CHUNK // 2 // PIECE
        self.halves = x_ref.shape[0] // (CHUNK // 2)

    def part(self, ref, p):
        return ref.at[pl.ds(pl.multiple_of(p * PIECE, PIECE), PIECE), :]

    def right(self, src, p):
        return pltpu.make_async_remote_copy(
            src_ref=self.part(src, p), dst_ref=self.part(self.from_left, p), send_sem=self.sr.at[p], recv_sem=self.rl.at[p],
            device_id={"tp": jnp.minimum(self.me + 1, self.size - 1)}, device_id_type=MESH)

    def left(self, src, p):
        return pltpu.make_async_remote_copy(
            src_ref=self.part(src, p), dst_ref=self.part(self.from_right, p), send_sem=self.sl.at[p], recv_sem=self.rr.at[p],
            device_id={"tp": jnp.maximum(self.me - 1, 0)}, device_id_type=MESH)

    def order(self, half):
        return half

    def send_own(self, step):
        @pl.when(self.me == 0)
        def _():
            @pl.loop(0, 2 * self.half)
            def _(k):
                self.right(self.x, self.order(2 * step) * self.half + k).start()

        @pl.when(self.me == self.size - 1)
        def _():
            @pl.loop(0, 2 * self.half)
            def _(k):
                self.left(self.x, self.order(2 * step) * self.half + k).start()

    def advance(self, tick):
        me, size, halves = self.me, self.size, self.halves
        hr = tick - 1 - self.lag * me
        hl = tick - 1 - self.lag * (size - 1 - me)
        hf = tick - 1 - self.lag * jnp.maximum(me, size - 1 - me)

        @pl.loop(0, self.half)
        def _(k):
            @pl.when((me > 0) & (hr >= 0) & (hr < halves))
            def _():
                p = hr * self.half + k
                self.right(self.to_right, p).wait_recv()

                @pl.when(me < size - 1)
                def _():
                    self.part(self.to_right, p)[...] = (
                        self.part(self.from_left, p)[...].astype(F32) + self.part(self.x, p)[...].astype(F32)).astype(BF16)
                    self.right(self.to_right, p).start()

            @pl.when((me < size - 1) & (hl >= 0) & (hl < halves))
            def _():
                p = hl * self.half + k
                self.left(self.to_left, p).wait_recv()

                @pl.when(me > 0)
                def _():
                    self.part(self.to_left, p)[...] = (
                        self.part(self.from_right, p)[...].astype(F32) + self.part(self.x, p)[...].astype(F32)).astype(BF16)
                    self.left(self.to_left, p).start()

            @pl.when((hf >= 0) & (hf < halves))
            def _():
                p = hf * self.half + k
                own = self.part(self.x, p)[...].astype(F32)

                @pl.when(me == 0)
                def _():
                    self.part(self.sum, p)[...] = own + self.part(self.from_right, p)[...].astype(F32)

                @pl.when(me == size - 1)
                def _():
                    self.part(self.sum, p)[...] = own + self.part(self.from_left, p)[...].astype(F32)

                @pl.when((me > 0) & (me < size - 1))
                def _():
                    self.part(self.sum, p)[...] = (
                        own + self.part(self.from_left, p)[...].astype(F32) + self.part(self.from_right, p)[...].astype(F32))

    def finish(self, step):
        @pl.when(step == self.blocks - 1)
        def _():
            @pl.loop(self.halves, self.halves + 1 + self.lag * (self.size - 1))
            def _(tick):
                self.advance(tick)

            @pl.loop(0, self.halves * self.half)
            def _(p):
                @pl.when(self.me < self.size - 1)
                def _():
                    self.right(self.to_right, p).wait_send()

                @pl.when(self.me > 0)
                def _():
                    self.left(self.to_left, p).wait_send()


class StreamGather:
    def __init__(self, size, pieces, x_ref, out_ref, own_sem, sl, sr, rl, rr):
        self.size, self.pieces = size, pieces
        self.me = lax.axis_index("tp")
        self.x, self.out, self.own_sem = x_ref, out_ref, own_sem
        self.sl, self.sr, self.rl, self.rr = sl, sr, rl, rr
        self.shard = x_ref.shape[0]
        self.rows = self.shard // pieces

    def region(self, s, k):
        return self.out.at[pl.ds(pl.multiple_of(s * self.shard + k * self.rows, self.rows), self.rows), :]

    def to_right(self, src, s, k):
        return pltpu.make_async_remote_copy(
            src_ref=src, dst_ref=self.region(s, k), send_sem=self.sr.at[s * self.pieces + k], recv_sem=self.rl.at[s * self.pieces + k],
            device_id={"tp": jnp.minimum(self.me + 1, self.size - 1)}, device_id_type=MESH)

    def to_left(self, src, s, k):
        return pltpu.make_async_remote_copy(
            src_ref=src, dst_ref=self.region(s, k), send_sem=self.sl.at[s * self.pieces + k], recv_sem=self.rr.at[s * self.pieces + k],
            device_id={"tp": jnp.maximum(self.me - 1, 0)}, device_id_type=MESH)

    def own(self):
        here = pl.ds(pl.multiple_of(self.me * self.shard, self.shard), self.shard)
        return pltpu.make_async_copy(self.x, self.out.at[here, :], self.own_sem)

    def start(self):
        self.own().start()
        for k in range(self.pieces):
            src = self.x.at[pl.ds(k * self.rows, self.rows), :]

            @pl.when(self.me < self.size - 1)
            def _():
                self.to_right(src, self.me, k).start()

            @pl.when(self.me > 0)
            def _():
                self.to_left(src, self.me, k).start()

    def tick(self, t):
        d = t // self.pieces + 1
        k = t % self.pieces
        s_left, s_right = self.me - d, self.me + d

        @pl.when((t >= 0) & (d < self.size) & (s_left >= 0))
        def _():
            self.to_right(self.region(s_left, k), s_left, k).wait_recv()

            @pl.when(self.me < self.size - 1)
            def _():
                self.to_right(self.region(s_left, k), s_left, k).start()

        @pl.when((t >= 0) & (d < self.size) & (s_right < self.size))
        def _():
            self.to_left(self.region(s_right, k), s_right, k).wait_recv()

            @pl.when(self.me > 0)
            def _():
                self.to_left(self.region(s_right, k), s_right, k).start()

    def finish(self, steps):
        @pl.loop(steps - 1, max((self.size - 1) * self.pieces, steps - 1))
        def _(t):
            self.tick(t)

        self.own().wait()

        @pl.loop(0, self.size * self.pieces)
        def _(t):
            s, k = t // self.pieces, t % self.pieces

            @pl.when((self.me < self.size - 1) & (s <= self.me))
            def _():
                self.to_right(self.region(s, k), s, k).wait_send()

            @pl.when((self.me > 0) & (s >= self.me))
            def _():
                self.to_left(self.region(s, k), s, k).wait_send()


def stream_scratch(rows, width):
    buf = pltpu.VMEM((rows, width), BF16)
    dma = pltpu.SemaphoreType.DMA((rows // PIECE,))
    return [buf, buf, buf, buf, buf, dma, dma, dma, dma]


def fwd_kernel(
    size, lag, heads, dk, dv, tokens_ref, norm_gain_ref, taps_ref, misc_ref, gain_ref, out_w_ref, shard_ref,
    normed_ref, proj_ref, gated_ref, mixed_ref, u_ref, inv_ref, start_ref, sum_ref, whole_ref, landed, own_sem, gsl, gsr, grl, grr, ext_ref, state_ref, x_ref, *line_refs
):
    rows = CHUNK
    step = pl.program_id(0)
    line = StreamSum(size, lag, pl.num_programs(0), x_ref, sum_ref, *line_refs)
    gather = StreamGather(size, 2, shard_ref, landed, own_sem, gsl, gsr, grl, grr)
    kw, vw = heads * dk, heads * dv
    conv_w = 2 * kw + vw

    @pl.when(step == 0)
    def _():
        line_barrier(line.me, size)
        gather.start()
        ext_ref[0:8, :] = jnp.zeros((8, conv_w), F32)
        state_ref[...] = jnp.zeros_like(state_ref)

    values = tokens_ref[...].astype(F32)
    normed = (values * lax.rsqrt(jnp.mean(values * values, axis=-1, keepdims=True) + epsilon) * norm_gain_ref[...]).astype(BF16)
    normed_ref[...] = normed
    proj_ref[...] = mm(normed, out_w_ref[0 : conv_w + vw + 128, :], NT)
    ext_ref[pl.ds(8, rows), :] = proj_ref[:, 0:conv_w]
    conv = conv_rows(ext_ref, taps_ref, rows)
    ext_ref[0:8, :] = ext_ref[pl.ds(rows, 8), :]
    act = conv * sigmoid(conv)
    logits = logits_act(proj_ref[:, conv_w + vw :], misc_ref, heads)
    cum, cum_t = decay_tables(logits, heads)
    row = grid_index((rows, rows), 0)
    col = grid_index((rows, rows), 1)
    for h in range(heads):
        q, _ = unit_rows(act[:, h * dk : (h + 1) * dk], dk ** (-0.5))
        k, _ = unit_rows(act[:, kw + h * dk : kw + (h + 1) * dk], 1.0)
        v = act[:, 2 * kw + h * dv : 2 * kw + (h + 1) * dv].astype(BF16).astype(F32)
        q, k = q.astype(BF16), k.astype(BF16)
        beta = logits[:, h : h + 1]
        g_col = cum[:, heads + h : heads + h + 1]
        g_row = cum_t[heads + h : heads + h + 1, :]
        decay = jnp.where(row >= col, jnp.exp(jnp.where(row >= col, g_col - g_row, 0.0)), 0.0)
        grams = mm(jnp.concatenate([k, q], axis=0), k, NT)
        system = jnp.where(row > col, decay * grams[:rows], 0.0) * beta
        scores = decay * grams[rows:]
        inverse = unit_inverse(system)
        growth = jnp.exp(g_col)
        g_last = g_row[:, rows - 1 : rows]
        tail = jnp.exp(g_last - g_col)
        state = state_ref[:, h * dv : (h + 1) * dv]
        start_ref[0, :, h * dv : (h + 1) * dv] = state.astype(start_ref.dtype)
        seen = mm(jnp.concatenate([k, q], axis=0), state)
        u = mm(inverse, beta * (v - growth * seen[:rows]))
        mixed = growth * seen[rows:] + mm(scores, u)
        state_ref[:, h * dv : (h + 1) * dv] = jnp.exp(g_last) * state + mm(k, tail * u, TN)
        cols = slice(h * dv, (h + 1) * dv)
        mixed_ref[:, cols] = mixed
        u_ref[:, cols] = u.astype(u_ref.dtype)
        inv_ref[:, h * rows : (h + 1) * rows] = inverse.astype(inv_ref.dtype)
        gate = proj_ref[:, conv_w + h * dv : conv_w + (h + 1) * dv]
        scale = lax.rsqrt(jnp.mean(mixed * mixed, axis=-1, keepdims=True) + epsilon)
        gated = (mixed * scale * gain_ref[:, cols] * gate * sigmoid(gate)).astype(BF16)
        gated_ref[:, cols] = gated
        part = mm(gated, out_w_ref[conv_w + vw + 128 + h * dv : conv_w + vw + 128 + (h + 1) * dv, :])
        branch = part if h == 0 else branch + part
        if h == 0:
            line.advance(2 * step)
    gather.tick(step - 1)
    x_ref[pl.ds(pl.multiple_of(step * rows, rows), rows), :] = branch.astype(BF16)
    line.send_own(step)
    line.advance(2 * step + 1)
    line.finish(step)

    @pl.when(step == pl.num_programs(0) - 1)
    def _():
        gather.finish(total_steps(tokens_ref, sum_ref))
        whole_ref[...] = landed[...]


def total_steps(block_ref, whole_ref):
    return whole_ref.shape[0] // block_ref.shape[0]


def mixer_fwd(tokens, norm_gain, taps, misc, gain, out_w, shard, heads, dk, dv, size, lag, collective_id):
    total_rows = tokens.shape[0]
    chunks = total_rows // CHUNK
    vw = heads * dv
    conv_w = 2 * heads * dk + vw
    model = out_w.shape[1]
    width = conv_w + vw + 128
    blk = lambda w: pl.BlockSpec((CHUNK, w), lambda c: (c, 0))
    full = lambda a: pl.BlockSpec(a.shape, lambda c: (0, 0))
    return pl.pallas_call(
        functools.partial(fwd_kernel, size, lag, heads, dk, dv),
        grid=(chunks,),
        in_specs=[blk(model), full(norm_gain), full(taps), full(misc), full(gain), full(out_w), full(shard)],
        out_specs=[
            blk(model), blk(width), blk(vw), blk(vw), blk(vw), blk(heads * CHUNK), pl.BlockSpec((1, dk, vw), lambda c: (c, 0, 0)),
            pl.BlockSpec((total_rows, model), lambda c: (0, 0)), pl.BlockSpec((total_rows, model), lambda c: (0, 0)),
        ],
        out_shape=[
            jax.ShapeDtypeStruct((total_rows, model), BF16),
            jax.ShapeDtypeStruct((total_rows, width), F32),
            jax.ShapeDtypeStruct((total_rows, vw), BF16),
            jax.ShapeDtypeStruct((total_rows, vw), F32),
            jax.ShapeDtypeStruct((total_rows, vw), BF16),
            jax.ShapeDtypeStruct((total_rows, heads * CHUNK), BF16),
            jax.ShapeDtypeStruct((chunks, dk, vw), BF16),
            jax.ShapeDtypeStruct((total_rows, model), F32),
            jax.ShapeDtypeStruct((total_rows, model), shard.dtype),
        ],
        scratch_shapes=[pltpu.VMEM((total_rows, model), BF16), pltpu.SemaphoreType.DMA] + [pltpu.SemaphoreType.DMA((size * 2,))] * 4
        + [pltpu.VMEM((8 + CHUNK, conv_w), F32), pltpu.VMEM((dk, vw), F32)] + stream_scratch(total_rows, model),
        compiler_params=pltpu.CompilerParams(collective_id=collective_id, has_side_effects=True),
        cost_estimate=cost(88),
        name="mixer_fwd",
    )(tokens, norm_gain, taps, misc, gain, out_w, shard)


def bwd_kernel(heads, dk, dv, out_grad_ref, sent_ref, w_ref, proj_ref, before_ref, taps_ref, misc_ref, gain_ref, mixed_ref, u_ref, inv_ref,
               start_ref, gbranch_ref, gproj_ref, tapg_ref, small_ref, gaing_ref, ext_ref, back_ref, dstate_ref):
    rows = CHUNK
    kw, vw = heads * dk, heads * dv
    conv_w = 2 * kw + vw
    step = pl.program_id(0)
    chunk = pl.num_programs(0) - 1 - step

    @pl.when(step == 0)
    def _():
        back_ref[pl.ds(rows, 8), :] = jnp.zeros((8, conv_w), F32)
        dstate_ref[...] = jnp.zeros_like(dstate_ref)
        tapg_ref[...] = jnp.zeros_like(tapg_ref)
        small_ref[...] = jnp.zeros_like(small_ref)
        gaing_ref[...] = jnp.zeros_like(gaing_ref)

    gbranch = (out_grad_ref[...].astype(F32) + sent_ref[...]).astype(BF16)
    gbranch_ref[...] = gbranch
    grad_gated = mm(gbranch, w_ref[conv_w + vw + 128 :, :], NT)
    ext_ref[0:8, :] = jnp.where(chunk > 0, before_ref[:, 0:conv_w], 0.0)
    ext_ref[pl.ds(8, rows), :] = proj_ref[:, 0:conv_w]
    conv = conv_rows(ext_ref, taps_ref, rows)
    sig = sigmoid(conv)
    act = conv * sig
    dact = sig * (1.0 + conv * (1.0 - sig))
    raw = proj_ref[:, conv_w + vw :]
    logits = logits_act(raw, misc_ref, heads)
    cum, cum_t = decay_tables(logits, heads)
    row = grid_index((rows, rows), 0)
    col = grid_index((rows, rows), 1)
    lane = col
    dlog = jnp.zeros((rows, rows), F32)
    for h in range(heads):
        cols = slice(h * dv, (h + 1) * dv)
        gate = proj_ref[:, conv_w + h * dv : conv_w + (h + 1) * dv]
        gsig = sigmoid(gate)
        mixed = mixed_ref[:, cols]
        grad = grad_gated[:, cols]
        gain = gain_ref[:, cols]
        scale = lax.rsqrt(jnp.mean(mixed * mixed, axis=-1, keepdims=True) + epsilon)
        unit = mixed * scale
        weighted = grad * gate * gsig
        gaing_ref[0:1, cols] += jnp.sum(weighted * unit, axis=0, keepdims=True)
        gproj_ref[:, conv_w + h * dv : conv_w + (h + 1) * dv] = (grad * gain * unit * gsig * (1.0 + gate * (1.0 - gsig))).astype(BF16)
        pulled = weighted * gain
        d_out = scale * (pulled - unit * jnp.mean(pulled * unit, axis=-1, keepdims=True))
        qs, ks = slice(h * dk, (h + 1) * dk), slice(kw + h * dk, kw + (h + 1) * dk)
        vs = slice(2 * kw + h * dv, 2 * kw + (h + 1) * dv)
        q_f, q_scale = unit_rows(act[:, qs], dk ** (-0.5))
        k_f, k_scale = unit_rows(act[:, ks], 1.0)
        v = act[:, vs].astype(BF16).astype(F32)
        q, k = q_f.astype(BF16), k_f.astype(BF16)
        q32, k32 = q.astype(F32), k.astype(F32)
        beta = logits[:, h : h + 1]
        g_col = cum[:, heads + h : heads + h + 1]
        g_row = cum_t[heads + h : heads + h + 1, :]
        decay = jnp.where(row >= col, jnp.exp(jnp.where(row >= col, g_col - g_row, 0.0)), 0.0)
        grams = mm(jnp.concatenate([k, q], axis=0), k, NT)
        plain = jnp.where(row > col, decay * grams[:rows], 0.0)
        scores = decay * grams[rows:]
        growth = jnp.exp(g_col)
        g_last = g_row[:, rows - 1 : rows]
        tail = jnp.exp(g_last - g_col)
        inverse = inv_ref[:, h * rows : (h + 1) * rows]
        u = u_ref[:, cols]
        start = start_ref[0, :, cols]
        d_end = dstate_ref[:, cols]
        d_end_b = d_end.astype(BF16)
        d_u = mm(scores, d_out, TN) + tail * mm(k, d_end_b)
        d_rhs = mm(inverse, d_u, TN)
        d_seen = -growth * d_rhs
        g_out = growth * d_out
        both = mm(jnp.concatenate([d_rhs, d_out], axis=0), u, NT)
        d_sys = jnp.where(row > col, -both[:rows], 0.0)
        d_scores = jnp.where(row >= col, both[rows:], 0.0)
        dstate_ref[:, cols] = jnp.exp(g_last) * d_end + mm(jnp.concatenate([k, q], axis=0), jnp.concatenate([beta * d_seen, g_out], axis=0), TN)
        pull = mm(jnp.concatenate([d_seen, g_out], axis=0), start, NT)
        d_k_seen, d_q1 = pull[:rows], pull[rows:]
        d_k_tail = tail * mm(u, d_end_b, NT)
        d_qk = d_scores * decay
        d_gram = d_sys * decay * beta
        d_gram = d_gram + jnp.transpose(d_gram)
        near = mm(jnp.concatenate([d_qk, d_gram], axis=0), k)
        d_q = d_q1 + near[:rows]
        d_k = beta * d_k_seen + d_k_tail + near[rows:] + mm(d_qk, q, TN)
        d_v = beta * d_rhs
        seen_dot = jnp.sum(k32 * d_k_seen, axis=-1, keepdims=True)
        tail_dot = jnp.sum(k32 * d_k_tail, axis=-1, keepdims=True)
        sys_plain = d_sys * plain
        d_beta = jnp.sum(sys_plain, axis=-1, keepdims=True) + jnp.sum(d_rhs * v, axis=-1, keepdims=True) + seen_dot
        mixed_terms = sys_plain * beta + d_scores * scores
        d_cum = (
            jnp.sum(mixed_terms, axis=-1, keepdims=True)
            - jnp.sum(jnp.transpose(mixed_terms), axis=-1, keepdims=True)
            + beta * seen_dot
            - tail_dot
            + jnp.sum(q32 * d_q1, axis=-1, keepdims=True)
        )
        d_last = jnp.sum(tail_dot, axis=0, keepdims=True) + jnp.exp(g_last) * jnp.sum(
            jnp.sum(d_end * start.astype(F32), axis=-1, keepdims=True), axis=0, keepdims=True
        )
        d_cum = d_cum + jnp.where(grid_index((rows, 1), 0) == rows - 1, d_last, 0.0)
        dlog = jnp.where(lane == h, d_beta, jnp.where(lane == heads + h, d_cum, dlog))
        q_hat, k_hat = q_f * dk**0.5, k_f
        d_q = d_q * dk ** (-0.5)
        d_qa = q_scale * (d_q - q_hat * jnp.sum(d_q * q_hat, axis=-1, keepdims=True))
        d_ka = k_scale * (d_k - k_hat * jnp.sum(d_k * k_hat, axis=-1, keepdims=True))
        back_ref[0:rows, qs] = d_qa * dact[:, qs]
        back_ref[0:rows, ks] = d_ka * dact[:, ks]
        back_ref[0:rows, vs] = d_v * dact[:, vs]
    tri = jnp.where(row <= col, 1.0, 0.0)
    d_decay = mm_exact(tri, dlog)
    shifted = sigmoid(raw + misc_ref[1:2, :])
    d_raw = jnp.where(lane < heads, dlog * logits * (1.0 - logits), d_decay * misc_ref[0:1, :] * shifted)
    d_raw = jnp.where(lane < 2 * heads, d_raw, 0.0)
    gproj_ref[:, conv_w + vw :] = d_raw.astype(BF16)
    small_ref[0:1, :] += jnp.sum(d_decay * logits, axis=0, keepdims=True)
    small_ref[1:2, :] += jnp.sum(d_raw, axis=0, keepdims=True)
    here = back_ref[0:rows, :]
    total = taps_ref[0:1, :] * here
    tapg_ref[0:1, :] += jnp.sum(here * ext_ref[pl.ds(8, rows), :], axis=0, keepdims=True)
    for offset in range(1, 4):
        total = total + taps_ref[offset : offset + 1, :] * back_ref[pl.ds(offset, rows), :]
        tapg_ref[offset : offset + 1, :] += jnp.sum(here * ext_ref[pl.ds(8 - offset, rows), :], axis=0, keepdims=True)
    gproj_ref[:, 0:conv_w] = total.astype(BF16)
    back_ref[pl.ds(rows, 8), :] = back_ref[0:8, :]


def mixer_bwd(out_grad, sent, w_rows, proj, taps, misc, gain, mixed, u, inverse, start, heads, dk, dv):
    total_rows, width = proj.shape
    chunks = total_rows // CHUNK
    conv_w = 2 * heads * dk + heads * dv
    vw = heads * dv
    last = chunks - 1
    model = out_grad.shape[1]
    blk = lambda w: pl.BlockSpec((CHUNK, w), lambda c: (last - c, 0))
    full = lambda a: pl.BlockSpec(a.shape, lambda c: (0, 0))
    per = CHUNK // 8
    return pl.pallas_call(
        functools.partial(bwd_kernel, heads, dk, dv),
        grid=(chunks,),
        in_specs=[
            blk(model), blk(model), full(w_rows), blk(width),
            pl.BlockSpec((8, width), lambda c: (jnp.maximum((last - c) * per - 1, 0), 0)),
            full(taps), full(misc), full(gain), blk(vw), blk(vw), blk(heads * CHUNK),
            pl.BlockSpec((1, dk, vw), lambda c: (last - c, 0, 0)),
        ],
        out_specs=[
            blk(model), blk(width),
            pl.BlockSpec((8, conv_w), lambda c: (0, 0)),
            pl.BlockSpec((8, 128), lambda c: (0, 0)),
            pl.BlockSpec((8, vw), lambda c: (0, 0)),
        ],
        out_shape=[
            jax.ShapeDtypeStruct((total_rows, model), BF16),
            jax.ShapeDtypeStruct((total_rows, width), BF16),
            jax.ShapeDtypeStruct((8, conv_w), F32),
            jax.ShapeDtypeStruct((8, 128), F32),
            jax.ShapeDtypeStruct((8, vw), F32),
        ],
        scratch_shapes=[
            pltpu.VMEM((8 + CHUNK, conv_w), F32),
            pltpu.VMEM((CHUNK + 8, conv_w), F32),
            pltpu.VMEM((dk, vw), F32),
        ],
        cost_estimate=cost(27),
        name="mixer_bwd",
    )(out_grad, sent, w_rows, proj, proj, taps, misc, gain, mixed, u, inverse, start)


def ff_kernel(
    size, lag, wide, tokens_ref, branch_ref, grad_ref, gain_ref, w_ref, normed_ref, inner_ref, acts_ref, part_ref, gaing_ref, sum_ref, x_ref, *line_refs
):
    rows = CHUNK
    step = pl.program_id(0)
    line = StreamSum(size, lag, pl.num_programs(0), x_ref, sum_ref, *line_refs)

    @pl.when(step == 0)
    def _():
        line_barrier(line.me, size)
        gaing_ref[...] = jnp.zeros_like(gaing_ref)

    hidden = (tokens_ref[...].astype(F32) + branch_ref[...]).astype(BF16).astype(F32)
    scale = lax.rsqrt(jnp.mean(hidden * hidden, axis=-1, keepdims=True) + epsilon)
    unit = hidden * scale
    normed = (unit * gain_ref[...]).astype(BF16)
    normed_ref[...] = normed
    gate = mm(normed, w_ref[0:wide, :], NT)
    up = mm(normed, w_ref[wide : 2 * wide, :], NT)
    sig = sigmoid(gate)
    inner = (gate * sig * up).astype(BF16)
    inner_ref[...] = inner
    part_ref[...] = mm(inner, w_ref[2 * wide : 3 * wide, :]).astype(BF16)
    line.advance(2 * step)
    grad_inner = mm(grad_ref[...], w_ref[2 * wide : 3 * wide, :], NT)
    grad_gate = (grad_inner * up * sig * (1.0 + gate * (1.0 - sig))).astype(BF16)
    grad_up = (grad_inner * gate * sig).astype(BF16)
    acts_ref[:, 0:wide] = grad_gate
    acts_ref[:, wide : 2 * wide] = grad_up
    grad_normed = mm(grad_gate, w_ref[0:wide, :]) + mm(grad_up, w_ref[wide : 2 * wide, :])
    gaing_ref[0:1, :] += jnp.sum(grad_normed * unit, axis=0, keepdims=True)
    pulled = grad_normed * gain_ref[...]
    sent = scale * (pulled - unit * jnp.mean(pulled * unit, axis=-1, keepdims=True))
    x_ref[pl.ds(pl.multiple_of(step * rows, rows), rows), :] = sent.astype(BF16)
    line.send_own(step)
    line.advance(2 * step + 1)
    line.finish(step)


def feed_forward(tokens, branch, grad, gain, w_rows, wide, size, lag, collective_id):
    total_rows, model = tokens.shape
    chunks = total_rows // CHUNK
    blk = lambda w: pl.BlockSpec((CHUNK, w), lambda c: (c, 0))
    full = lambda r, w: pl.BlockSpec((r, w), lambda c: (0, 0))
    return pl.pallas_call(
        functools.partial(ff_kernel, size, lag, wide),
        grid=(chunks,),
        in_specs=[blk(model), blk(model), blk(model), full(1, model), full(3 * wide, model)],
        out_specs=[blk(model), blk(wide), blk(2 * wide), blk(model), full(8, model), full(total_rows, model)],
        out_shape=[
            jax.ShapeDtypeStruct((total_rows, model), BF16),
            jax.ShapeDtypeStruct((total_rows, wide), BF16),
            jax.ShapeDtypeStruct((total_rows, 2 * wide), BF16),
            jax.ShapeDtypeStruct((total_rows, model), BF16),
            jax.ShapeDtypeStruct((8, model), F32),
            jax.ShapeDtypeStruct((total_rows, model), F32),
        ],
        scratch_shapes=stream_scratch(total_rows, model),
        compiler_params=pltpu.CompilerParams(collective_id=collective_id, has_side_effects=True),
        cost_estimate=cost(65),
        name="feed_forward",
    )(tokens, branch, grad, gain, w_rows)


def peer_barrier(fsdp, tp):
    me_f, me_t = lax.axis_index("fsdp"), lax.axis_index("tp")
    barrier = pltpu.get_barrier_semaphore()

    @pl.loop(1, fsdp)
    def _(d):
        pl.semaphore_signal(barrier, inc=1, device_id={"fsdp": (me_f + d) % fsdp}, device_id_type=MESH)

    @pl.loop(1, tp)
    def _(d):
        pl.semaphore_signal(barrier, inc=1, device_id={"tp": (me_t + d) % tp}, device_id_type=MESH)

    pl.semaphore_wait(barrier, fsdp + tp - 2)


def line_gather_kernel(fsdp, size, pieces, x_ref, tile_ref, out_ref, tiles_ref, own_sem, sl, sr, rl, rr, sp, rp, st, rt):
    me = lax.axis_index("tp")
    shard = x_ref.shape[0]
    rows = shard // pieces
    own = pltpu.make_async_copy(x_ref, out_ref.at[pl.ds(pl.multiple_of(me * shard, shard), shard), :], own_sem)
    own.start()
    me_f = lax.axis_index("fsdp")
    tiles_ref[pl.ds(me_f, 1), pl.ds(me, 1)] = tile_ref[...][None, None]
    peer_barrier(fsdp, size)

    def along(d, slot):
        return pltpu.make_async_remote_copy(
            src_ref=tile_ref, dst_ref=tiles_ref.at[me_f, slot], send_sem=st.at[d], recv_sem=rt.at[slot],
            device_id={"tp": (me + d) % size}, device_id_type=MESH)

    def across(d, slot):
        return pltpu.make_async_remote_copy(
            src_ref=tiles_ref.at[me_f], dst_ref=tiles_ref.at[slot], send_sem=sp.at[d], recv_sem=rp.at[slot],
            device_id={"fsdp": (me_f + d) % fsdp}, device_id_type=MESH)

    @pl.loop(1, size)
    def _(d):
        along(d, me).start()

    def region(ref, s, k):
        return ref.at[pl.ds(pl.multiple_of(s * shard + k * rows, rows), rows), :]

    def to_right(src, s, k):
        return pltpu.make_async_remote_copy(
            src_ref=src, dst_ref=region(out_ref, s, k), send_sem=sr.at[s * pieces + k], recv_sem=rl.at[s * pieces + k],
            device_id={"tp": jnp.minimum(me + 1, size - 1)}, device_id_type=MESH)

    def to_left(src, s, k):
        return pltpu.make_async_remote_copy(
            src_ref=src, dst_ref=region(out_ref, s, k), send_sem=sl.at[s * pieces + k], recv_sem=rr.at[s * pieces + k],
            device_id={"tp": jnp.maximum(me - 1, 0)}, device_id_type=MESH)

    for k in range(pieces):
        src = x_ref.at[pl.ds(k * rows, rows), :]

        @pl.when(me < size - 1)
        def _():
            to_right(src, me, k).start()

        @pl.when(me > 0)
        def _():
            to_left(src, me, k).start()

    @pl.loop(1, size)
    def _(d):
        along(d, (me + d) % size).wait_recv()

    @pl.loop(1, fsdp)
    def _(d):
        across(d, me_f).start()

    @pl.loop(0, (size - 1) * pieces)
    def _(t):
        d = t // pieces + 1
        k = t % pieces
        s_left, s_right = me - d, me + d

        @pl.when(s_left >= 0)
        def _():
            to_right(region(out_ref, s_left, k), s_left, k).wait_recv()

            @pl.when(me < size - 1)
            def _():
                to_right(region(out_ref, s_left, k), s_left, k).start()

        @pl.when(s_right < size)
        def _():
            to_left(region(out_ref, s_right, k), s_right, k).wait_recv()

            @pl.when(me > 0)
            def _():
                to_left(region(out_ref, s_right, k), s_right, k).start()

    own.wait()

    @pl.loop(1, fsdp)
    def _(d):
        across(d, (me_f + d) % fsdp).wait_recv()

    @pl.loop(1, size)
    def _(d):
        along(d, me).wait_send()

    @pl.loop(1, fsdp)
    def _(d):
        across(d, me_f).wait_send()

    @pl.loop(0, size * pieces)
    def _(t):
        s, k = t // pieces, t % pieces

        @pl.when((me < size - 1) & (s <= me))
        def _():
            to_right(region(out_ref, s, k), s, k).wait_send()

        @pl.when((me > 0) & (s >= me))
        def _():
            to_left(region(out_ref, s, k), s, k).wait_send()


def line_gather(x, tile, fsdp, size, pieces, collective_id):
    vm = pl.BlockSpec(memory_space=pltpu.VMEM)
    dma = pltpu.SemaphoreType.DMA((size * pieces,))
    plane, line = pltpu.SemaphoreType.DMA((fsdp,)), pltpu.SemaphoreType.DMA((size,))
    return pl.pallas_call(
        functools.partial(line_gather_kernel, fsdp, size, pieces),
        out_shape=[
            jax.ShapeDtypeStruct((size * x.shape[0], x.shape[1]), x.dtype),
            jax.ShapeDtypeStruct((fsdp, size) + tile.shape, tile.dtype),
        ],
        in_specs=[vm, vm], out_specs=[vm, vm],
        scratch_shapes=[pltpu.SemaphoreType.DMA, dma, dma, dma, dma, plane, plane, line, line],
        compiler_params=pltpu.CompilerParams(collective_id=collective_id, has_side_effects=True),
        cost_estimate=cost(40),
        name="line_gather",
    )(x, tile)


class PlaneSum:
    def __init__(self, n, order, cols, src_ref, out_ref, acc_ref, recv_ref, send_sem, recv_sem):
        self.n, self.order, self.cols = n, order, cols
        self.stages = len(order)
        self.me = lax.axis_index("fsdp")
        self.block = src_ref.shape[0] // n
        self.src, self.out, self.acc, self.recv = src_ref, out_ref, acc_ref, recv_ref
        self.send_sem, self.recv_sem = send_sem, recv_sem

    def bit(self, b):
        return (self.me // b) % 2

    def owner(self, stage, i, flip):
        total = 0
        for b in self.order[:stage]:
            total = total + self.bit(b) * b
        b = self.order[stage]
        total = total + ((1 - self.bit(b)) if flip else self.bit(b)) * b
        for j, r in enumerate(self.order[stage + 1 :]):
            total = total + ((i // (2**j)) % 2) * r
        return total

    def place(self, pair):
        total = 0
        for j, r in enumerate(self.order[1:]):
            total = total + ((pair // (r // 2)) % 2) * 2**j
        return total

    def rows(self, g):
        return pl.ds(pl.multiple_of(g * self.block, self.block), self.block)

    def copy(self, stage, i):
        b = self.order[stage]
        src = self.src if stage == 0 else self.acc
        slot = self.n - (self.n >> stage) + i
        return pltpu.make_async_remote_copy(
            src_ref=src.at[self.rows(self.owner(stage, i, True)), self.cols], dst_ref=self.recv.at[self.rows(slot), self.cols],
            send_sem=self.send_sem.at[slot], recv_sem=self.recv_sem.at[slot],
            device_id={"fsdp": self.me + b - 2 * b * self.bit(b)}, device_id_type=MESH)

    def total(self, stage, i):
        self.copy(stage, i).wait_recv()
        g = self.owner(stage, i, False)
        slot = self.n - (self.n >> stage) + i
        src = self.src if stage == 0 else self.acc
        return g, src[self.rows(g), self.cols].astype(F32) + self.recv[self.rows(slot), self.cols].astype(F32)

    def advance(self, stage):
        if stage == self.stages - 1:
            _, total = self.total(stage, 0)
            self.out[:, self.cols] = total
            return
        mine = self.bit(self.order[stage + 1])
        for flip in (True, False):
            @pl.loop(0, self.n >> (stage + 2))
            def _(i):
                g, total = self.total(stage, 2 * i + (1 - mine if flip else mine))
                self.acc[self.rows(g), self.cols] = total.astype(BF16)
                if flip:
                    self.copy(stage + 1, i).start()

    def advance_pair(self, pair):
        i = self.place(pair)
        g, total = self.total(0, i)
        self.acc[self.rows(g), self.cols] = total.astype(BF16)

        @pl.when(i % 2 != self.bit(self.order[1]))
        def _():
            self.copy(1, i // 2).start()

    def finish(self):
        @pl.loop(0, self.n // 2)
        def _(i):
            self.copy(0, i).wait_send()

        for stage in range(1, self.stages):
            @pl.loop(0, self.n >> (stage + 1))
            def _(i):
                self.copy(stage, i).wait_send()


def halving_orders(n):
    bits = [2**j for j in range(n.bit_length() - 1)]
    return bits, bits[:1] + bits[:0:-1]


def last_kernel(
    fsdp, size, pieces, slack, gproj_ref, w_ref, normed_ref, tokens_ref, gain_ref, gbranch_ref, gated_ref, base_ref, small_ref, tapg_ref,
    out_ref, small_out, tap_out, shard_ref,
    x_ref, grads, acc, recv, small, small_in, small_line, tap_in, from_left, from_right, to_left, to_right,
    sl, sr, rl, rr, sp, rp, st, rt, sk, rk, sa, ra, sb, rb
):
    me, me_f = lax.axis_index("tp"), lax.axis_index("fsdp")
    shard = x_ref.shape[0] // size
    rows = shard // pieces
    count = (size - 1) * pieces
    proj_w = gproj_ref.shape[1]
    peer_barrier(fsdp, size)

    def across(d, slot):
        return pltpu.make_async_remote_copy(
            src_ref=small, dst_ref=small_in.at[slot], send_sem=sp.at[d], recv_sem=rp.at[slot],
            device_id={"fsdp": (me_f + d) % fsdp}, device_id_type=MESH)

    def taps_across(d, slot):
        return pltpu.make_async_remote_copy(
            src_ref=tapg_ref, dst_ref=tap_in.at[slot], send_sem=sk.at[d], recv_sem=rk.at[slot],
            device_id={"fsdp": (me_f + d) % fsdp}, device_id_type=MESH)

    def along(d, slot):
        return pltpu.make_async_remote_copy(
            src_ref=small_out, dst_ref=small_line.at[slot], send_sem=st.at[d], recv_sem=rt.at[slot],
            device_id={"tp": (me + d) % size}, device_id_type=MESH)

    width = grads.shape[1]
    cut = (width // 256 + width // 128 % 2) * 128
    order_a, order_b = halving_orders(fsdp)
    planes = [
        PlaneSum(fsdp, order_a, slice(0, cut), grads, shard_ref, acc, recv, sa, ra),
        PlaneSum(fsdp, order_b, slice(cut, width), grads, shard_ref, acc, recv, sb, rb),
    ]

    def part(ref, s, k):
        return ref.at[pl.ds(pl.multiple_of(s * shard + k * rows, rows), rows), :]

    def right_copy(src, s, k):
        return pltpu.make_async_remote_copy(
            src_ref=part(src, s, k), dst_ref=part(from_left, s, k), send_sem=sr.at[s * pieces + k], recv_sem=rl.at[s * pieces + k],
            device_id={"tp": jnp.minimum(me + 1, size - 1)}, device_id_type=MESH)

    def left_copy(src, s, k):
        return pltpu.make_async_remote_copy(
            src_ref=part(src, s, k), dst_ref=part(from_right, s, k), send_sem=sl.at[s * pieces + k], recv_sem=rr.at[s * pieces + k],
            device_id={"tp": jnp.maximum(me - 1, 0)}, device_id_type=MESH)

    def exchange(t):
        ir = t - (me - 1) * slack
        il = t - (size - 2 - me) * slack
        s_r, k_r = size - 1 - ir // pieces, ir % pieces
        s_l, k_l = il // pieces, il % pieces

        @pl.when((me > 0) & (ir >= 0) & (ir < count) & (s_r >= me))
        def _():
            right_copy(to_right, s_r, k_r).wait_recv()

            @pl.when(s_r > me)
            def _():
                part(to_right, s_r, k_r)[...] = (
                    part(from_left, s_r, k_r)[...].astype(F32) + part(x_ref, s_r, k_r)[...].astype(F32)).astype(BF16)
                right_copy(to_right, s_r, k_r).start()

        @pl.when((me < size - 1) & (il >= 0) & (il < count) & (s_l <= me))
        def _():
            left_copy(to_left, s_l, k_l).wait_recv()

            @pl.when(s_l < me)
            def _():
                part(to_left, s_l, k_l)[...] = (
                    part(from_right, s_l, k_l)[...].astype(F32) + part(x_ref, s_l, k_l)[...].astype(F32)).astype(BF16)
                left_copy(to_left, s_l, k_l).start()

    small[...] = small_ref[...]

    @pl.loop(0, size)
    def _(j):
        s = (j % 2) * (j // 2) + (1 - j % 2) * (size - 1 - j // 2)
        here = pl.ds(pl.multiple_of(s * shard, shard), shard)
        grad_normed = mm(gproj_ref[here, :], w_ref[0:proj_w, :])
        values = tokens_ref[here, :].astype(F32)
        scale = lax.rsqrt(jnp.mean(values * values, axis=-1, keepdims=True) + epsilon)
        unit = values * scale
        small[0:1, :] += jnp.sum(grad_normed * unit, axis=0, keepdims=True)
        pulled = grad_normed * gain_ref[...]
        x_ref[here, :] = (scale * (pulled - unit * jnp.mean(pulled * unit, axis=-1, keepdims=True))).astype(BF16)

        @pl.when((me == 0) & (s > 0))
        def _():
            @pl.loop(0, pieces)
            def _(k):
                right_copy(x_ref, s, k).start()

        @pl.when((me == size - 1) & (s < size - 1))
        def _():
            @pl.loop(0, pieces)
            def _(k):
                left_copy(x_ref, s, k).start()

    @pl.loop(1, fsdp)
    def _(d):
        taps_across(d, me_f).start()
        across(d, me_f).start()

    block = grads.shape[0] // fsdp
    many = max(256 // block, 2)
    groups = fsdp // many
    ticks = count + (size - 2) * slack
    per = max(3 * ticks // (7 * groups), 1)
    pairs = many // 2

    def group_at(i):
        mine, other = me_f // many, groups - 1 - i
        total = 0
        for b in halving_orders(groups)[0]:
            total = total + ((mine // b + other // b) % 2) * b
        return total

    def advance_group(i):
        @pl.loop(0, pairs)
        def _(m):
            for plane in planes:
                plane.advance_pair(group_at(i) * pairs + m)

    @pl.loop(0, groups)
    def _(i):
        g = group_at(i)
        here = pl.ds(pl.multiple_of(g * many * block, many * block), many * block)
        grads[here, 0:proj_w] = mm(normed_ref[:, here], gproj_ref[...], TN).astype(BF16)
        grads[here, proj_w:width] = mm(gbranch_ref[:, here], gated_ref[...], TN).astype(BF16)

        @pl.loop(0, pairs)
        def _(m):
            for plane in planes:
                plane.copy(0, plane.place(g * pairs + m)).start()

        @pl.loop(i * per, (i + 1) * per)
        def _(t):
            exchange(t)

        @pl.when(i > 0)
        def _():
            advance_group(i - 1)

    advance_group(groups - 1)
    stages = len(order_a)
    done = groups * per
    for stage in range(stages):
        if stage > 0:
            until = max(done, int(ticks * (0.45 + 0.3 * (stage - 1) / max(stages - 2, 1))))

            @pl.loop(done, until)
            def _(t):
                exchange(t)

            done = until
            for plane in planes:
                plane.advance(stage)
        if stage == 0:
            small_out[...] = small[...]
            tap_out[...] = tapg_ref[...]

            @pl.loop(1, fsdp)
            def _(d):
                slot = (me_f + d) % fsdp
                across(d, slot).wait_recv()
                taps_across(d, slot).wait_recv()
                small_out[...] += small_in[pl.ds(slot, 1)][0]
                tap_out[...] += tap_in[pl.ds(slot, 1)][0]

            @pl.loop(1, size)
            def _(d):
                along(d, me).start()

    @pl.loop(done, ticks)
    def _(t):
        exchange(t)

    for plane in planes:
        plane.finish()

    @pl.loop(1, size)
    def _(d):
        along(d, me).wait_send()

    @pl.loop(1, size)
    def _(d):
        slot = (me + d) % size
        along(d, slot).wait_recv()
        small_out[...] += small_line[pl.ds(slot, 1)][0]

    @pl.loop(1, fsdp)
    def _(d):
        across(d, me_f).wait_send()
        taps_across(d, me_f).wait_send()

    @pl.loop(0, pieces)
    def _(k):
        here = pl.ds(pl.multiple_of(k * rows, rows), rows)
        total = base_ref[here, :] + part(x_ref, me, k)[...].astype(F32)

        @pl.when(me == 0)
        def _():
            out_ref[here, :] = total + part(from_right, me, k)[...].astype(F32)

        @pl.when(me == size - 1)
        def _():
            out_ref[here, :] = total + part(from_left, me, k)[...].astype(F32)

        @pl.when((me > 0) & (me < size - 1))
        def _():
            out_ref[here, :] = total + part(from_left, me, k)[...].astype(F32) + part(from_right, me, k)[...].astype(F32)

    @pl.loop(0, size * pieces)
    def _(i):
        s, k = i // pieces, i % pieces

        @pl.when(s > me)
        def _():
            right_copy(to_right, s, k).wait_send()

        @pl.when(s < me)
        def _():
            left_copy(to_left, s, k).wait_send()


def last_sums(gproj, w_rows, normed, tokens, gain, gbranch, gated, base, small, tapg, fsdp, size, pieces, slack, collective_id):
    vm = pl.BlockSpec(memory_space=pltpu.VMEM)
    total_rows, model = tokens.shape
    width = gproj.shape[1] + gated.shape[1]
    buf = pltpu.VMEM((total_rows, model), BF16)
    pack = pltpu.VMEM((model, width), BF16)
    dma = pltpu.SemaphoreType.DMA((size * pieces,))
    plane, line = pltpu.SemaphoreType.DMA((fsdp,)), pltpu.SemaphoreType.DMA((size,))
    return pl.pallas_call(
        functools.partial(last_kernel, fsdp, size, pieces, slack),
        out_shape=[
            jax.ShapeDtypeStruct(base.shape, F32), jax.ShapeDtypeStruct(small.shape, F32), jax.ShapeDtypeStruct(tapg.shape, F32),
            jax.ShapeDtypeStruct((model // fsdp, width), F32),
        ],
        in_specs=[vm] * 10, out_specs=[vm] * 4,
        scratch_shapes=[
            buf, pack, pack, pack, pltpu.VMEM(small.shape, F32), pltpu.VMEM((fsdp,) + small.shape, F32), pltpu.VMEM((size,) + small.shape, F32),
            pltpu.VMEM((fsdp,) + tapg.shape, F32), buf, buf, buf, buf,
            dma, dma, dma, dma, plane, plane, line, line, plane, plane, plane, plane, plane, plane,
        ],
        compiler_params=pltpu.CompilerParams(collective_id=collective_id, has_side_effects=True),
        cost_estimate=cost(55),
        name="last_sums",
    )(gproj, w_rows, normed, tokens, gain, gbranch, gated, base, small, tapg)


def norm_scale(values):
    return lax.rsqrt(jnp.mean(values * values, axis=-1, keepdims=True) + epsilon)


def norm_back(grad_normed, values, scale, gain):
    unit = values * scale
    gain_grad = jnp.sum(grad_normed * unit, axis=0)
    pulled = grad_normed * gain
    input_part = scale * (pulled - unit * jnp.mean(pulled * unit, axis=-1, keepdims=True))
    return (input_part, gain_grad)


def body(
    tokens, lengths, gain_mix, w_query, w_key, w_value, w_outgate, w_beta, w_decay,
    conv_query, conv_key, conv_value, decay_log, decay_bias, gain_head, w_out, gain_ff,
    w_gate, w_up, w_down, cotangent,
):
    fsdp, tp = lax.axis_size("fsdp"), lax.axis_size("tp")
    my_fsdp, my_tp = lax.axis_index("fsdp"), lax.axis_index("tp")
    shard_rows, d_model = tokens.shape
    w_rows = w_query.shape[0]
    heads = w_beta.shape[1]
    kw, vw = w_query.shape[1], w_value.shape[1]
    dk, dv = kw // heads, vw // heads
    conv_w = 2 * kw + vw
    main_w = conv_w + vw
    proj_w = main_w + 128
    ff = w_gate.shape[1]
    taps_n = conv_query.shape[0]

    taps_local = jnp.concatenate([conv_query, conv_key, conv_value], axis=1).reshape(1, -1)
    spare = 128 - 2 * heads
    tap_rows = -(-taps_local.shape[1] // spare)
    taps_pack = jnp.pad(taps_local, ((0, 0), (0, tap_rows * spare - taps_local.shape[1]))).reshape(tap_rows, spare)
    taps_pack = jnp.pad(taps_pack, ((0, w_rows - tap_rows), (0, 0)))
    extras = jnp.concatenate([w_beta, w_decay, taps_pack], axis=1)
    mix_pack = jnp.concatenate([jnp.transpose(a) for a in (w_query, w_key, w_value, w_outgate, extras)] + [w_out], axis=0)
    mix_pack, tokens = lax.optimization_barrier((mix_pack, tokens))
    mix_full = lax.all_gather(mix_pack, "fsdp", axis=1, tiled=True)
    n_mix, n_head = gain_mix.shape[0], gain_head.shape[0]
    gains_local = jnp.concatenate([gain_mix, gain_head, gain_ff]).astype(F32)
    gains_tile = jnp.pad(gains_local[None, :], ((0, 7), (0, 128 - gains_local.shape[0])))
    group_tokens, gains = line_gather(tokens, gains_tile, fsdp, tp, 2, 4)
    gains = jnp.transpose(gains[:, :, 0, :], (1, 0, 2)).reshape(tp * fsdp, 128)
    mix_gain = gains[:, :n_mix].reshape(-1)
    head_gain = gains[:, n_mix : n_mix + n_head].reshape(-1)
    ff_gain = gains[:, n_mix + n_head : 2 * n_mix + n_head].reshape(-1)
    live = my_tp * shard_rows + jnp.arange(shard_rows, dtype=jnp.int32) < lengths[0]
    grad_out = jnp.where(live[:, None], cotangent, jnp.zeros_like(cotangent))
    wide = -(-ff // 128) * 128
    pad_wide = lambda a: jnp.pad(a, ((0, wide - ff), (0, 0)))
    ff_pack = jnp.concatenate([pad_wide(jnp.transpose(w_gate)), pad_wide(jnp.transpose(w_up)), pad_wide(w_down)], axis=0)

    taps_all = mix_full[main_w + 2 * heads : proj_w].reshape(spare, fsdp, w_rows)[:, :, :tap_rows]
    taps_all = jnp.transpose(taps_all, (1, 2, 0)).reshape(fsdp, -1)
    cq, cv = conv_query.shape[1], conv_value.shape[1]
    taps_all = taps_all[:, : taps_n * (2 * cq + cv)].reshape(fsdp, taps_n, 2 * cq + cv)
    taps_all = jnp.transpose(taps_all, (1, 0, 2))
    taps = jnp.concatenate(
        [taps_all[:, :, :cq].reshape(taps_n, -1), taps_all[:, :, cq : 2 * cq].reshape(taps_n, -1), taps_all[:, :, 2 * cq :].reshape(taps_n, -1)],
        axis=1,
    ).astype(F32)
    taps = jnp.pad(taps, ((0, 8 - taps_n), (0, 0)))
    log_f, bias_f = decay_log.astype(F32), decay_bias.astype(F32)
    pad_lanes = lambda v: jnp.pad(v, (heads, 128 - 2 * heads))[None, :]
    misc = jnp.pad(jnp.concatenate([pad_lanes(-jnp.exp(log_f)), pad_lanes(bias_f)], axis=0), ((0, 6), (0, 0)))
    gain_row = jnp.tile(head_gain, heads)[None, :]

    normed, proj, gated, mixed, u, inverse, start, branch, group_grad_ff = mixer_fwd(
        group_tokens, mix_gain[None, :], taps, misc, gain_row, mix_full, grad_out, heads, dk, dv, tp, 2, 3)
    ff_full = lax.all_gather(ff_pack, "fsdp", axis=1, tiled=True)
    own_rows = lambda full: lax.dynamic_slice_in_dim(full, my_tp * shard_rows, shard_rows, axis=0)
    hidden_state = tokens.astype(F32) + own_rows(branch)

    ff_normed, inner, grad_acts, ff_part, ff_gain_grad, sent_sum = feed_forward(
        group_tokens, branch, group_grad_ff, ff_gain[None, :], ff_full, wide, tp, 2, 5)
    ff_gain_grad = ff_gain_grad[0]
    ff_weight_grad = lax.dot_general(ff_normed, grad_acts, TN, preferred_element_type=F32)
    down_grad = lax.dot_general(group_grad_ff, inner, TN, preferred_element_type=F32)
    ff_grads = jnp.concatenate([ff_weight_grad.astype(BF16), down_grad.astype(BF16)], axis=1)
    sent_sum, ff_grads = lax.optimization_barrier((sent_sum, ff_grads))
    ff_sums = lax.psum_scatter(ff_grads, "fsdp", scatter_dimension=0, tiled=True).astype(F32)
    ff_branch = lax.psum_scatter(ff_part, "tp", scatter_dimension=0, tiled=True)
    grad_hidden = grad_out.astype(F32) + own_rows(sent_sum)

    group_grad_branch, grad_projected, tap_grads, small, head_gain_grad = mixer_bwd(
        group_grad_ff, sent_sum, mix_full, proj, taps, misc, gain_row, mixed, u, inverse, start, heads, dk, dv
    )
    ff_branch, grad_projected = lax.optimization_barrier((ff_branch, grad_projected))
    head_part = jnp.sum(head_gain_grad[0].reshape(heads, dv), axis=0)
    decays = jnp.pad(jnp.concatenate([small[0, : 2 * heads], small[1, : 2 * heads]]), (0, 128 - 4 * heads))
    decays = jnp.where(jnp.arange(tp)[:, None] == my_tp, decays[None, :], 0.0).reshape(-1)
    others = jnp.pad(jnp.concatenate([head_part, decays]), (0, d_model - dv - tp * 128))
    small_rows = jnp.pad(jnp.stack([ff_gain_grad, others]), ((1, 5), (0, 0)))
    layer_out = jnp.where(live[:, None], hidden_state + ff_branch.astype(F32), 0.0).astype(BF16)
    input_grad, small_sums, tap_sums, mix_sums = last_sums(
        grad_projected, mix_full, normed, group_tokens, mix_gain[None, :], group_grad_branch, gated,
        grad_hidden, small_rows, tap_grads, fsdp, tp, 8, 2, 8)
    place = my_tp * fsdp + my_fsdp
    at = lambda row, start, n: lax.dynamic_slice(small_sums, (row, start), (1, n))[0]
    gain_mix_grad = at(0, place * n_mix, n_mix)
    gain_ff_grad = at(1, place * n_mix, n_mix)
    gain_head_grad = at(2, place * n_head, n_head)
    decay_sums = at(2, dv + my_tp * 128, 128)
    tap_at = lambda start, n: lax.dynamic_slice(tap_sums, (0, start + my_fsdp * n), (taps_n, n))
    return (
        layer_out,
        input_grad,
        gain_mix_grad,
        mix_sums[:, :kw],
        mix_sums[:, kw : 2 * kw],
        mix_sums[:, 2 * kw : conv_w],
        mix_sums[:, conv_w:main_w],
        mix_sums[:, main_w : main_w + heads],
        mix_sums[:, main_w + heads : main_w + 2 * heads],
        tap_at(0, cq),
        tap_at(kw, cq),
        tap_at(2 * kw, cv),
        decay_sums[heads : 2 * heads],
        decay_sums[3 * heads : 4 * heads],
        gain_head_grad,
        jnp.transpose(mix_sums[:, proj_w:]),
        gain_ff_grad,
        ff_sums[:, :ff],
        ff_sums[:, wide : wide + ff],
        jnp.transpose(ff_sums[:, 2 * wide : 2 * wide + ff]),
    )


def solution(mesh):
    placed = (
        P(("fsdp", "tp"), None),
        P("fsdp"),
        P(("tp", "fsdp")),
        P("fsdp", "tp"),
        P("fsdp", "tp"),
        P("fsdp", "tp"),
        P("fsdp", "tp"),
        P("fsdp", "tp"),
        P("fsdp", "tp"),
        P(None, ("tp", "fsdp")),
        P(None, ("tp", "fsdp")),
        P(None, ("tp", "fsdp")),
        P("tp"),
        P("tp"),
        P(("tp", "fsdp")),
        P("tp", "fsdp"),
        P(("tp", "fsdp")),
        P("fsdp", "tp"),
        P("fsdp", "tp"),
        P("tp", "fsdp"),
        P(("fsdp", "tp"), None),
    )
    return jax.shard_map(
        body,
        mesh=mesh,
        in_specs=placed,
        out_specs=(
            P(("fsdp", "tp"), None),
            P(("fsdp", "tp"), None),
            P(("tp", "fsdp")),
            P("fsdp", "tp"),
            P("fsdp", "tp"),
            P("fsdp", "tp"),
            P("fsdp", "tp"),
            P("fsdp", "tp"),
            P("fsdp", "tp"),
            P(None, ("tp", "fsdp")),
            P(None, ("tp", "fsdp")),
            P(None, ("tp", "fsdp")),
            P("tp"),
            P("tp"),
            P(("tp", "fsdp")),
            P("tp", "fsdp"),
            P(("tp", "fsdp")),
            P("fsdp", "tp"),
            P("fsdp", "tp"),
            P("tp", "fsdp"),
        ),
        check_vma=False,
    )
```
